32 devices in a mesh: tok: 16 (over z, x, core), fsdp: 2 (over y).
Axes of the slice: x: 2, y: 2, z: 4, core: 2. Of those that a mesh axis runs over, the one named last changes fastest.
Arguments:
- qkv: bfloat16 [12288, 3, 3072], P('tok', None, 'fsdp'), may hold values from -42 to 42
- prefix_kv: bfloat16 [2, 2048, 3072], P(None, 'tok', 'fsdp'), may hold values from -9 to 9
- cache_pool: bfloat16 [16, 16, 2, 128, 3072], P('tok', None, None, None, 'fsdp'), may hold values from -9 to 9
- page_table: int32 [16, 16], P('tok'), may hold values from 0 to 15, each once within a row
- cached_lens: int32 [16], P('tok'), may hold values from 0 to 2048, as said below
- span_lens: int32 [16], P('tok'), may hold values from 192 to 768, as said below
- dense_weight: bfloat16 [3072, 6144], P(None, 'fsdp'), may hold values from -0.625 to 0.625
- dense_bias: float32 [6144], P('fsdp'), may hold values from -1.8 to 1.8
Outputs:
- attended: bfloat16 [12288, 6144], P('tok', 'fsdp')
The draws below stay inside these ranges and needn't reach their ends.
Inputs may be any that keep to these rules, and one draw needn't show every extreme that they name: `page_table`: each row names each of the prompt's 16 stored pages once. `cached_lens`: some prompt has a full cache and some none. `span_lens`: some prompt fills all 768 slots, some a quarter of them.
All inputs are finite; a program needn't handle non-finite values.
Results may differ from the reference program's by a relative error of at most 0.0075.
Values may be sent and summed in bfloat16 or wider, within the bound.
No kernel may reach another device: no remote copies, remote signals or barrier semaphores. Data moves between devices by JAX's collectives and lax.ppermute only.
A program may use at most 320 MiB of HBM per device.

```python
import jax
import jax.numpy as jnp
from jax import lax

D = 6144
H = 32
HD = 96
ROT = 24
PAGE = 128
MAXP = 16
SPAN = 768
HF = 3072
PROMPTS = 16
PREFIX = 2048
TOKENS = 12288


def draw_qkv(key, part):
    return jnp.clip(1.5 * jax.random.normal(key, (TOKENS, 3, HF), jnp.float32), -9.0, 9.0).astype(jnp.bfloat16)


def draw_cached_lens(key, part):
    most_len = MAXP * PAGE
    lengths = jax.random.randint(key, (PROMPTS,), 0, most_len + 1, jnp.int32)
    chosen = jax.random.randint(jax.random.fold_in(key, 7), (), 0, PROMPTS, jnp.int32)
    lengths = lengths.at[chosen].set(most_len)
    return lengths.at[(chosen + 1) % PROMPTS].set(0)


def draw_span_lens(key, part):
    lengths = jax.random.randint(key, (PROMPTS,), SPAN // 4, SPAN + 1, jnp.int32)
    chosen = jax.random.randint(jax.random.fold_in(key, 11), (), 0, PROMPTS, jnp.int32)
    lengths = lengths.at[chosen].set(SPAN)
    return lengths.at[(chosen + 1) % PROMPTS].set(SPAN // 4)


def block_levels(rng, extent, split, least, top_value):
    level, own = 1.0, jax.random.fold_in(rng, 6)
    for dim, blocks in split:
        heights = jnp.exp(jax.random.uniform(jax.random.fold_in(own, dim), (blocks,), jnp.float32, least / len(split), top_value / len(split)))
        level = level * jnp.repeat(heights, extent[dim] // blocks).reshape([-1 if axis == dim else 1 for axis in range(len(extent))])
    return level


def bell_draw(own_key, extent, spread, most, pieces=(), kind=jnp.bfloat16):
    entries = spread * jax.random.normal(own_key, extent, jnp.float32)
    if pieces:
        entries = entries * block_levels(own_key, extent, pieces, -0.22, 0.18)
    return jnp.clip(entries, -most, most).astype(kind)


def setup_inputs(seed: int = 0) -> dict:
    splits = jax.random.split(jax.random.key(seed), 9)
    qkv = draw_qkv(jax.random.fold_in(splits[8], 71), 0)
    prefix_kv = bell_draw(splits[1], (2, PREFIX, HF), 1.5, 9.0, ((1, 16), (2, 2)))
    cache_pool = bell_draw(splits[2], (PROMPTS, MAXP, 2, PAGE, HF), 1.5, 9.0, ((0, 16), (4, 2)))
    page_table = jax.vmap(lambda own: jax.random.permutation(own, MAXP))(jax.random.split(splits[3], PROMPTS)).reshape((PROMPTS, MAXP)).astype(jnp.int32)
    cached_lens = draw_cached_lens(jax.random.fold_in(splits[8], 71), 0)
    span_lens = draw_span_lens(jax.random.fold_in(splits[8], 71), 0)
    dense_weight = bell_draw(splits[6], (HF, D), (HF // 32) ** -0.5, 0.625, ((1, 2),))
    dense_bias = bell_draw(splits[7], (D,), 0.3, 1.8, ((0, 2),), jnp.float32)
    return {"qkv": qkv, "prefix_kv": prefix_kv, "cache_pool": cache_pool, "page_table": page_table, "cached_lens": cached_lens, "span_lens": span_lens, "dense_weight": dense_weight, "dense_bias": dense_bias}


def rotate_heads(tensor, positions):
    half_rot = ROT // 2
    inverse_freq = jnp.power(10000.0, -jnp.arange(half_rot, dtype=jnp.float32) * 2.0 / ROT)
    angles = positions.astype(jnp.float32)[:, None] * inverse_freq[None, :]
    cosine = jnp.cos(angles)[:, None, :]
    sine_val = jnp.sin(angles)[:, None, :]
    front_part = tensor[..., :half_rot]
    back_part = tensor[..., half_rot:ROT]
    return jnp.concatenate([front_part * cosine - back_part * sine_val, back_part * cosine + front_part * sine_val, tensor[..., ROT:]], axis=-1)


def reference(qkv, prefix_kv, cache_pool, page_table, cached_lens, span_lens, dense_weight, dense_bias):
    score_scale = HD ** -0.5
    row_ids = jnp.arange(SPAN, dtype=jnp.int32)

    def one_prompt(inputs):
        prompt_qkv, page_pool, page_order, cached, live_rows = inputs
        positions = PREFIX + cached + row_ids

        def with_rotary(tensor):
            turned = rotate_heads(tensor.astype(jnp.float32).reshape(SPAN, H, HD), positions)
            return turned.reshape(SPAN, HF).astype(jnp.bfloat16)

        queries = with_rotary(prompt_qkv[:, 0])
        new_keys = with_rotary(prompt_qkv[:, 1])
        new_values = prompt_qkv[:, 2]
        pages = page_pool[page_order]
        cache_keys = pages[:, 0].reshape(MAXP * PAGE, HF)
        cache_values = pages[:, 1].reshape(MAXP * PAGE, HF)
        key_rows = jnp.concatenate([prefix_kv[0], cache_keys, new_keys], axis=0)
        value_rows = jnp.concatenate([prefix_kv[1], cache_values, new_values], axis=0)
        slot_pos = jnp.arange(MAXP * PAGE, dtype=jnp.int32)
        allowed = jnp.concatenate([
            jnp.ones((SPAN, PREFIX), jnp.bool_),
            jnp.broadcast_to((slot_pos < cached)[None, :], (SPAN, MAXP * PAGE)),
            row_ids[None, :] <= row_ids[:, None]], axis=1)

        def one_head(head_idx):
            start_col = (head_idx * HD).astype(jnp.int32)
            query_head = lax.dynamic_slice_in_dim(queries, start_col, HD, 1)
            key_head = lax.dynamic_slice_in_dim(key_rows, start_col, HD, 1)
            value_head = lax.dynamic_slice_in_dim(value_rows, start_col, HD, 1)
            scores = jnp.dot(query_head, key_head.T, preferred_element_type=jnp.float32) * score_scale
            scores = jnp.where(allowed, scores, -1e30)
            row_top = jnp.max(scores, axis=1, keepdims=True)
            weights = jnp.where(allowed, jnp.exp(scores - row_top), 0.0)
            row_total = jnp.sum(weights, axis=1, keepdims=True)
            mixed = jnp.dot(weights.astype(jnp.bfloat16), value_head, preferred_element_type=jnp.float32)
            return mixed / row_total

        per_head = lax.map(one_head, jnp.arange(H, dtype=jnp.int32))
        context = jnp.transpose(per_head, (1, 0, 2)).reshape(SPAN, HF).astype(jnp.bfloat16)
        result = jnp.dot(context, dense_weight, preferred_element_type=jnp.float32) + dense_bias.astype(jnp.float32)[None, :]
        result = jnp.where((row_ids < live_rows)[:, None], result, 0.0)
        return result.astype(jnp.bfloat16)

    outputs = lax.map(one_prompt, (qkv.reshape(PROMPTS, SPAN, 3, HF), cache_pool, page_table, cached_lens, span_lens))
    return outputs.reshape(TOKENS, D)
```

```python
import functools
import math

import jax
import jax.numpy as jnp
from jax import lax
from jax.experimental import pallas as pl
from jax.experimental.pallas import tpu as pltpu
from jax.sharding import PartitionSpec as P

HD = 96
ROT = 24
LANES = 128
GROUP = 4
GW = GROUP * HD
NEG = -1e30
f32, bf16 = jnp.float32, jnp.bfloat16
SCALE = HD ** -0.5 * math.log2(math.e)
WIN = ((0, 128), (0, 256), (128, 256), (256, 128))
ONES = (127, 0, 255, 0)
TOPS = (126, 1, 254, 1)
STEP = 128


def attend_kernel(scal, *rest, local, prefix, piece, span, page_len, max_pages, bq, bk, U):
    it = iter(rest)
    if local:
        qkv, pool, table = next(it), next(it), next(it)
    else:
        qh, st = next(it), next(it)
    pieces = [next(it) for _ in piece] if prefix else []
    if prefix:
        out = next(it)
    if local:
        qh = next(it)
        if not prefix:
            st = next(it)
        qk, tb, sem_q, sem_c = next(it), next(it), next(it), next(it)
    kb, vb, ve = next(it), next(it), next(it)
    if prefix:
        ctx, sem_p = next(it), next(it)
    cached = scal[0]
    live = scal[1]
    cols = pl.ds(pl.multiple_of(scal[2], LANES), GW)
    pcol = pl.ds(pl.multiple_of(scal[3], LANES), GW)
    n_pages = pl.cdiv(cached, page_len)
    base_c = span if local else 0
    base_p = span + max_pages * page_len if local else 0
    per = bk // page_len
    n_cb = pl.cdiv(cached, bk)
    n_full = cached // bk

    def add_ones(at):
        r = pl.ds(at, STEP)
        lane = lax.broadcasted_iota(jnp.int32, (STEP, LANES), 1)
        v0 = vb[r, 0:128]
        v2 = vb[r, 256:384]
        one = jnp.ones((STEP, LANES), bf16)
        ve[r, 0:128] = jnp.where(lane == 127, one, v0)
        ve[r, 128:256] = jnp.where(lane == 0, one, v2)
        vb[r, 0:128] = jnp.where(lane == 0, one, v0)
        vb[r, 256:384] = jnp.where(lane == 127, one, v2)

    if local:
        new_copies = [
            pltpu.make_async_copy(qkv.at[0, :, cols], qk.at[0], sem_q.at[0]),
            pltpu.make_async_copy(qkv.at[1, :, cols], qk.at[1], sem_q.at[1]),
            pltpu.make_async_copy(qkv.at[2, :, cols], vb.at[pl.ds(0, span), :], sem_q.at[2]),
            pltpu.make_async_copy(table, tb, sem_q.at[3]),
        ]
        for c in new_copies:
            c.start()

        def page_copies(g):
            dst = pl.ds(pl.multiple_of(base_c + g * page_len, page_len), page_len)
            return (pltpu.make_async_copy(pool.at[scal[4 + g], 0, :, cols], kb.at[dst, :], sem_c.at[0, g]),
                    pltpu.make_async_copy(pool.at[scal[4 + g], 1, :, cols], vb.at[dst, :], sem_c.at[1, g]))

        def start_page(g, c):
            for x in page_copies(g):
                x.start()
            return c
        lax.fori_loop(0, n_pages, start_page, 0)

    def piece_copies(i):
        at, n = piece[i]
        dst = pl.ds(base_p + at, n)
        return (pltpu.make_async_copy(pieces[i].at[0, :, pcol], kb.at[dst, :], sem_p.at[0, i]),
                pltpu.make_async_copy(pieces[i].at[1, :, pcol], vb.at[dst, :], sem_p.at[1, i]))

    if prefix:
        for i in range(len(piece)):
            for x in piece_copies(i):
                x.start()

    if local:
        for c in new_copies:
            c.wait()

        def prep_new(j, c):
            at = pl.multiple_of(j * STEP, STEP)
            r = pl.ds(at, STEP)
            lane = lax.broadcasted_iota(jnp.int32, (STEP, GW), 1)

            def turn(x):
                x = x.astype(f32)
                return (x * tb[0, r, :] + pltpu.roll(x, GW - ROT // 2, 1) * tb[1, r, :]
                        + pltpu.roll(x, ROT // 2, 1) * tb[2, r, :]).astype(bf16)
            q = turn(qk[0, r, :])
            kb[r, :] = turn(qk[1, r, :])
            for h, (lo, n) in enumerate(WIN):
                keep = (lane >= h * HD) & (lane < (h + 1) * HD)
                qh[h, r, 0:n] = jnp.where(keep, q, jnp.zeros_like(q))[:, lo:lo + n]
            add_ones(at)
            return c
        lax.fori_loop(0, pl.cdiv(live, bq) * (bq // STEP), prep_new, 0)

        def prep_page(g, c):
            at = pl.multiple_of(base_c + g * page_len, page_len)

            @pl.when(g < n_pages)
            def _():
                for x in page_copies(g):
                    x.wait()

            @pl.when(g >= n_pages)
            def _():
                vb[pl.ds(at, page_len), :] = jnp.zeros((page_len, GW), bf16)
            add_ones(at)
            return c
        lax.fori_loop(0, n_cb * per, prep_page, 0)

    if prefix:
        for i in range(len(piece)):
            for x in piece_copies(i):
                x.wait()
        total_p = sum(n for _, n in piece)

        def prep_prefix(j, c):
            add_ones(pl.multiple_of(base_p + j * STEP, STEP))
            return c
        lax.fori_loop(0, total_p // STEP, prep_prefix, 0)

    def dots(q, h, start, n):
        lo, w = WIN[h]
        return lax.dot_general(q, kb[pl.ds(start, n), lo:lo + w], (((1,), (1,)), ((), ())), preferred_element_type=f32)

    def weigh(p, h, start, n):
        lo, w = WIN[h]
        v = vb[pl.ds(start, n), lo:lo + w] if w == 256 else ve[pl.ds(start, n), (h // 3) * 128:(h // 3) * 128 + 128]
        return jnp.dot(p, v, preferred_element_type=f32)

    def fold(state, s, h, start, n):
        m, acc = state
        new = jnp.maximum(m, jnp.max(s, axis=1, keepdims=True))
        p = jnp.exp2((s - new) * SCALE).astype(bf16)
        return new, acc * jnp.exp2((m - new) * SCALE) + weigh(p, h, start, n)

    for qt in range(span // bq):
        @pl.when(qt * bq < live)
        def _():
            rows = pl.ds(qt * bq, bq)
            for h0 in range(0, GROUP, U):
                hs = list(range(h0, h0 + U))
                qs = [qh[h, rows, 0:WIN[h][1]] for h in hs]
                if local:
                    states = []
                    n_new = (qt + 1) * bq
                    ss = [dots(q, h, 0, n_new) for q, h in zip(qs, hs)]
                    ri = lax.broadcasted_iota(jnp.int32, (bq, bq), 0)
                    ci = lax.broadcasted_iota(jnp.int32, (bq, bq), 1)
                    for h, s in zip(hs, ss):
                        diag = jnp.where(ci <= ri, s[:, qt * bq:], NEG)
                        s = jnp.concatenate([s[:, :qt * bq], diag], axis=1) if qt else diag
                        m = jnp.max(s, axis=1, keepdims=True)
                        p = jnp.exp2((s - m) * SCALE).astype(bf16)
                        states.append((m, weigh(p, h, 0, n_new)))

                    def cache_block(masked, j, sts):
                        start = pl.multiple_of(base_c + j * bk, math.gcd(base_c, bk))
                        ss = [dots(q, h, start, bk) for q, h in zip(qs, hs)]
                        if masked:
                            ok = lax.broadcasted_iota(jnp.int32, (bq, bk), 1) < cached - j * bk
                            ss = [jnp.where(ok, s, NEG) for s in ss]
                        return tuple(fold(sx, s, h, start, bk) for sx, s, h in zip(sts, ss, hs))
                    states = lax.fori_loop(0, n_full, functools.partial(cache_block, False), tuple(states))
                    states = list(lax.fori_loop(n_full, n_cb, functools.partial(cache_block, True), states))
                else:
                    accs = [st[h, rows, 0:WIN[h][1]] for h in hs]
                    states = [(a[:, TOPS[h]:TOPS[h] + 1], a) for a, h in zip(accs, hs)]
                if prefix:
                    nb = total_p // bk
                    ss = [dots(q, h, base_p, bk) for q, h in zip(qs, hs)]
                    for j in range(nb):
                        nxt = ([dots(q, h, base_p + (j + 1) * bk, bk) for q, h in zip(qs, hs)]
                               if j + 1 < nb else None)
                        states = [fold(sx, s, h, base_p + j * bk, bk) for sx, s, h in zip(states, ss, hs)]
                        ss = nxt
                    for h, (m, acc) in zip(hs, states):
                        ctx[h, :, 0:WIN[h][1]] = acc / acc[:, ONES[h]:ONES[h] + 1]
                else:
                    for h, (m, acc) in zip(hs, states):
                        w = WIN[h][1]
                        lane = lax.broadcasted_iota(jnp.int32, (bq, w), 1)
                        st[h, rows, 0:w] = jnp.where(lane == TOPS[h], m, acc)
            if prefix:
                lane = lax.broadcasted_iota(jnp.int32, (bq, LANES), 1)
                out[rows, 0:128] = jnp.where(lane < 96, ctx[0, :, 0:128], ctx[1, :, 0:128]).astype(bf16)
                out[rows, 128:256] = jnp.where(lane < 64, ctx[1, :, 128:256], ctx[2, :, 0:128]).astype(bf16)
                out[rows, 256:384] = jnp.where(lane < 32, ctx[2, :, 128:256], ctx[3, :, 0:128]).astype(bf16)


def attend(scal, span, page_len, max_pages, local=None, carry=None, pieces=None, bq=384, bk=1024, U=2):
    info, at = [], 0
    for p in pieces or []:
        info.append((at, p.shape[1]))
        at += p.shape[1]
    bq = bq if span % bq == 0 else math.gcd(span, 256)
    bk = math.gcd(bk, at) if pieces else bk
    bk = math.gcd(bk, max_pages * page_len)
    keys = (span + max_pages * page_len if local else 0) + at
    any_ = pl.BlockSpec(memory_space=pl.ANY)
    smem = pl.BlockSpec(memory_space=pltpu.SMEM)
    vmem = pl.BlockSpec(memory_space=pltpu.VMEM)
    heads = jax.ShapeDtypeStruct((GROUP, span, 2 * LANES), bf16)
    state = jax.ShapeDtypeStruct((GROUP, span, 2 * LANES), f32)
    args, in_specs, outs, scratch = [scal], [smem], [], []
    if local:
        args += list(local)
        in_specs += [any_] * 3
    else:
        args += list(carry)
        in_specs += [vmem] * 2
    if pieces:
        args += list(pieces)
        in_specs += [any_] * len(pieces)
        outs.append(jax.ShapeDtypeStruct((span, GW), bf16))
    if local:
        if pieces:
            scratch.append(pltpu.VMEM(heads.shape, bf16))
        else:
            outs += [heads, state]
        scratch += [
            pltpu.VMEM((2, span, GW), bf16),
            pltpu.VMEM((3, span, GW), f32),
            pltpu.SemaphoreType.DMA((4,)),
            pltpu.SemaphoreType.DMA((2, max_pages)),
        ]
    scratch += [pltpu.VMEM((keys, GW), bf16), pltpu.VMEM((keys, GW), bf16), pltpu.VMEM((keys, 2 * LANES), bf16)]
    if pieces:
        scratch += [pltpu.VMEM((GROUP, bq, 2 * LANES), f32), pltpu.SemaphoreType.DMA((2, len(pieces)))]
    res = pl.pallas_call(
        functools.partial(attend_kernel, local=bool(local), prefix=bool(pieces), piece=info, span=span, page_len=page_len,
                          max_pages=max_pages, bq=bq, bk=bk, U=U),
        out_shape=outs,
        in_specs=in_specs,
        out_specs=[vmem] * len(outs),
        scratch_shapes=scratch,
        compiler_params=pltpu.CompilerParams(vmem_limit_bytes=56 << 20),
        cost_estimate=pl.CostEstimate(flops=8 * span * keys * GROUP * 2 * LANES, bytes_accessed=8 << 20,
                                      transcendentals=span * keys * GROUP),
        name="attend_" + "new" * bool(local) + "prefix" * bool(pieces),
    )(*args)
    return res[0] if pieces else tuple(res)


def project_kernel(scal, *rest, n, bq, depth):
    pieces, w, bias, out = rest[:n], rest[n], rest[n + 1], rest[n + 2]
    live = scal[0]
    span, cols = out.shape
    for qt in range(span // bq):
        rows = pl.ds(qt * bq, bq)

        @pl.when(qt * bq < live)
        def _():
            acc = jnp.broadcast_to(bias[...], (bq, cols))
            for i in range(n):
                acc = acc + jnp.dot(pieces[i][rows, :], w[pl.ds(pl.multiple_of(scal[1 + i], LANES), depth), :],
                                    preferred_element_type=f32)
            ok = lax.broadcasted_iota(jnp.int32, (bq, cols), 0) + qt * bq < live
            out[rows, :] = jnp.where(ok, acc, 0.0).astype(bf16)

        @pl.when(qt * bq >= live)
        def _():
            out[rows, :] = jnp.zeros((bq, cols), bf16)


def project(live, offsets, pieces, weight, bias):
    span, depth = pieces[0].shape
    k, cols = weight.shape
    bn = math.gcd(cols, 512)
    n = len(pieces)
    scal = jnp.stack([jnp.asarray(x, jnp.int32) for x in [live] + list(offsets)])
    return pl.pallas_call(
        functools.partial(project_kernel, n=n, bq=math.gcd(span, 256), depth=depth),
        grid=(cols // bn,),
        out_shape=jax.ShapeDtypeStruct((span, cols), bf16),
        in_specs=[pl.BlockSpec(memory_space=pltpu.SMEM)]
        + [pl.BlockSpec((span, depth), lambda j: (0, 0), pipeline_mode=pl.Buffered(1))] * n
        + [pl.BlockSpec((k, bn), lambda j: (0, j)), pl.BlockSpec((1, bn), lambda j: (0, j))],
        out_specs=pl.BlockSpec((span, bn), lambda j: (0, j)),
        compiler_params=pltpu.CompilerParams(vmem_limit_bytes=48 << 20),
        cost_estimate=pl.CostEstimate(flops=2 * span * k * cols, bytes_accessed=2 * (k * cols + span * (k + cols)),
                                      transcendentals=0),
        name="project",
    )(scal, *pieces, weight, bias.reshape(1, cols))


def rotary_table(positions):
    half = ROT // 2
    inv = jnp.power(10000.0, -jnp.arange(half, dtype=f32) * 2.0 / ROT)
    ang = positions.astype(f32)[:, None] * inv[None, :]
    cos, sin = jnp.cos(ang), jnp.sin(ang)
    n = positions.shape[0]
    one = jnp.ones((n, HD - ROT), f32)
    zero = jnp.zeros((n, HD - half), f32)
    return jnp.stack([
        jnp.tile(jnp.concatenate([cos, cos, one], 1), (1, GROUP)),
        jnp.tile(jnp.concatenate([-sin, zero], 1), (1, GROUP)),
        jnp.tile(jnp.concatenate([zero[:, :half], sin, zero[:, :HD - ROT]], 1), (1, GROUP))])


def chip_ring(chips):
    if chips == 8:
        return [2 * z for z in range(4)] + [2 * z + 1 for z in (3, 2, 1, 0)]
    return list(range(chips))


def after(x, *deps):
    return lax.optimization_barrier((x,) + deps)[0]


def local_fn(qkv, prefix_kv, cache_pool, page_table, cached_lens, span_lens, dense_weight, dense_bias):
    tok, fsdp = lax.axis_size("tok"), lax.axis_size("fsdp")
    span, _, width = qkv.shape
    qkv = jnp.transpose(qkv, (1, 0, 2))
    pool = cache_pool[0]
    max_pages, _, page_len, _ = pool.shape
    prefix_len = prefix_kv.shape[1] * tok
    f = lax.axis_index("fsdp")
    meta = jnp.concatenate([cached_lens, span_lens, page_table[0]])
    rows = jnp.arange(span, dtype=jnp.int32)

    def scalars(m, col, pcol):
        return jnp.concatenate([m[:2], jnp.stack([jnp.asarray(col, jnp.int32), jnp.asarray(pcol, jnp.int32)]), m[2:]])

    if width % (2 * GW) or tok % 2 or fsdp != 2:
        table = rotary_table(prefix_len + meta[0] + rows)
        whole = lax.all_gather(prefix_kv, "tok", axis=1, tiled=True)
        pieces, offsets = [], []
        for g in range(width // GW):
            got = attend(scalars(meta, g * GW, g * GW), span, page_len, max_pages, local=(qkv, pool, table), pieces=[whole])
            every = lax.all_gather(got, "fsdp", axis=0)
            for i in range(fsdp):
                pieces.append(every[i])
                offsets.append(i * width + g * GW)
        return project(meta[1], offsets, pieces, dense_weight, dense_bias)

    half = width // 2
    c = lax.axis_index("tok") % 2
    swap_pairs = [(i, i ^ 1) for i in range(tok)]
    ring = chip_ring(tok // 2)
    n = len(ring)
    ahead = [(2 * ring[i] + k, 2 * ring[(i + 1) % n] + k) for i in range(n) for k in range(2)]
    back = [(b, a) for a, b in ahead]

    def swap(x):
        return lax.ppermute(x, "tok", swap_pairs)

    def part(x, which):
        return lax.dynamic_slice_in_dim(x, which * half, half, x.ndim - 1)

    meta2 = swap(meta)
    mine = jnp.concatenate([part(prefix_kv, c), swap(part(prefix_kv, 1 - c))], axis=1)
    hop = {1: (lax.ppermute(mine, "tok", ahead), lax.ppermute(mine, "tok", back))}
    qkv2 = swap(part(qkv, 1 - c))
    pool2 = swap(part(pool, 1 - c))
    table = rotary_table(prefix_len + meta[0] + rows)
    table2 = rotary_table(prefix_len + meta2[0] + rows)
    own = (meta, qkv, pool, table, c * half)
    other = (meta2, qkv2, pool2, table2, 0)
    units = [(own, 0), (other, 0), (own, GW), (other, GW)] if half == 2 * GW else [
        (who, g * GW) for g in range(half // GW) for who in (own, other)]
    got = []
    steps = n // 2
    carries = []
    gate = []
    for i, (who, col) in enumerate(units):
        m, a, b, t, first = who
        s = after(scalars(m, first + col, col), *gate)
        carries.append((m, col, attend(s, span, page_len, max_pages, local=(a, b, t))))
        d = i + 2
        if d < steps:
            fw, bw = hop[d - 1]
            hop[d] = (lax.ppermute(fw, "tok", ahead), lax.ppermute(bw, "tok", back))
            gate = [fw[0, 0, 0], bw[0, 0, 0]]
        elif d == steps:
            fw, bw = hop[d - 1]
            k = fw.shape[1] // 2
            hop[d] = (lax.ppermute(fw[:, :k], "tok", ahead), lax.ppermute(bw[:, k:], "tok", back))
            gate = [fw[0, 0, 0], bw[0, 0, 0]]
        else:
            gate = []
    pieces = [mine] + [x for d in range(1, steps + 1) for x in hop[d]]
    proj, offsets = [], []
    ypairs = [(0, 1), (1, 0)]
    for i, (m, col, carry) in enumerate(carries):
        got = attend(scalars(m, 0, col), span, page_len, max_pages, carry=carry, pieces=pieces)
        at = c * half + col
        if i % 2:
            got = swap(got)
            at = (1 - c) * half + col
        proj += [got, lax.ppermute(got, "fsdp", ypairs)]
        offsets += [f * width + at, (1 - f) * width + at]
    return project(meta[1], offsets, proj, dense_weight, dense_bias)


def solution(mesh):
    return jax.shard_map(
        local_fn,
        mesh=mesh,
        in_specs=(
            P("tok", None, "fsdp"),
            P(None, "tok", "fsdp"),
            P("tok", None, None, None, "fsdp"),
            P("tok", None),
            P("tok"),
            P("tok"),
            P(None, "fsdp"),
            P("fsdp"),
        ),
        out_specs=P("tok", "fsdp"),
        check_vma=False,
    )
```

```python
import functools
import math

import jax
import jax.numpy as jnp
from jax import lax
from jax.experimental import pallas as pl
from jax.experimental.pallas import tpu as pltpu
from jax.sharding import PartitionSpec as P

HD = 96
ROT = 24
LANES = 128
GROUP = 4
GW = GROUP * HD
NEG = -1e30
f32, bf16 = jnp.float32, jnp.bfloat16
SCALE = HD ** -0.5 * math.log2(math.e)
SUM, TOP = HD, HD + 1
STEP = 128


def realign(x, h):
    lo = h * HD
    first = lo // LANES * LANES
    off = lo - first
    if off == 0:
        return x[:, first:first + LANES]
    if off + HD <= LANES:
        return pltpu.roll(x[:, first:first + LANES], LANES - off, 1)
    return pltpu.roll(x[:, first:first + 2 * LANES], 2 * LANES - off, 1)[:, :LANES]


def turn_tables(angles):
    half = ROT // 2
    row = lax.broadcasted_iota(jnp.int32, (ROT, LANES), 0)
    lane = lax.broadcasted_iota(jnp.int32, (ROT, LANES), 1)

    def pick(where_, sign=1.0):
        return jnp.dot(angles, jnp.where(where_, sign, 0.0), precision=lax.Precision.HIGHEST,
                       preferred_element_type=f32)
    here = pick((lane == row) & (row < half) | (lane == row + half) & (row < half))
    rest = lax.broadcasted_iota(jnp.int32, here.shape, 1) >= ROT
    return (jnp.where(rest, 1.0, here), pick((lane == row - half) & (row >= half), -1.0),
            pick((lane == row) & (row >= half)))


def attend_kernel(scal, *rest, local, prefix, piece, span, page_len, max_pages, bq, bk):
    it = iter(rest)
    if local:
        qkv, pool, angles = next(it), next(it), next(it)
    else:
        qh, st = next(it), next(it)
    pieces = [next(it) for _ in piece] if prefix else []
    if prefix:
        out = next(it)
    if local:
        qh = next(it)
        if not prefix:
            st = next(it)
        qk, sem_q, sem_c = next(it), next(it), next(it)
    kb, vb, kh, vh = next(it), next(it), next(it), next(it)
    if prefix:
        sem_p = next(it)
    cached = scal[0]
    live = scal[1]
    cols = pl.ds(pl.multiple_of(scal[2], LANES), GW)
    pcol = pl.ds(pl.multiple_of(scal[3], LANES), GW)
    n_pages = pl.cdiv(cached, page_len)
    base_c = span if local else 0
    base_p = span + max_pages * page_len if local else 0
    per = bk // page_len
    n_cb = pl.cdiv(cached, bk)
    n_full = cached // bk
    heads = range(GROUP)
    zero = jnp.zeros((STEP, LANES), bf16)

    def put_v(at, v):
        lane = lax.broadcasted_iota(jnp.int32, (STEP, LANES), 1)
        one = jnp.where(lane == SUM, 1.0, 0.0).astype(bf16)
        for h in heads:
            vh[h, pl.ds(at, STEP), :] = jnp.where(lane < HD, realign(v, h), one)

    def put_k(at, k):
        for h in heads:
            kh[h, pl.ds(at, STEP), :] = realign(k, h)

    if local:
        new_copies = [
            pltpu.make_async_copy(qkv.at[0, :, cols], qk.at[0], sem_q.at[0]),
            pltpu.make_async_copy(qkv.at[1, :, cols], qk.at[1], sem_q.at[1]),
            pltpu.make_async_copy(qkv.at[2, :, cols], vb.at[pl.ds(0, span), :], sem_q.at[2]),
        ]
        for c in new_copies:
            c.start()

        def page_copies(g):
            dst = pl.ds(pl.multiple_of(base_c + g * page_len, page_len), page_len)
            return (pltpu.make_async_copy(pool.at[scal[4 + g], 0, :, cols], kb.at[dst, :], sem_c.at[0, g]),
                    pltpu.make_async_copy(pool.at[scal[4 + g], 1, :, cols], vb.at[dst, :], sem_c.at[1, g]))

        def start_page(g, c):
            for x in page_copies(g):
                x.start()
            return c
        lax.fori_loop(0, n_pages, start_page, 0)

    def piece_copies(i):
        at, n = piece[i]
        dst = pl.ds(base_p + at, n)
        return (pltpu.make_async_copy(pieces[i].at[0, :, pcol], kb.at[dst, :], sem_p.at[0, i]),
                pltpu.make_async_copy(pieces[i].at[1, :, pcol], vb.at[dst, :], sem_p.at[1, i]))

    if prefix:
        for i in range(len(piece)):
            for x in piece_copies(i):
                x.start()

    if local:
        for c in new_copies:
            c.wait()

        def prep_new(j, c):
            at = pl.multiple_of(j * STEP, STEP)
            r = pl.ds(at, STEP)
            lane = lax.broadcasted_iota(jnp.int32, (STEP, LANES), 1)
            ta, tb, tc = turn_tables(angles[r, :])

            def turn(x, h):
                x = realign(x, h).astype(f32)
                x = x * ta + pltpu.roll(x, LANES - ROT // 2, 1) * tb + pltpu.roll(x, ROT // 2, 1) * tc
                return jnp.where(lane < HD, x, 0.0).astype(bf16)
            q, k = qk[0, r, :], qk[1, r, :]
            for h in heads:
                qh[h, r, :] = turn(q, h)
                kh[h, r, :] = turn(k, h)
            put_v(at, vb[r, :])
            return c
        lax.fori_loop(0, span // STEP, prep_new, 0)

        def prep_page(g, c):
            at = pl.multiple_of(base_c + g * page_len, page_len)

            @pl.when(g < n_pages)
            def _():
                for x in page_copies(g):
                    x.wait()
                put_k(at, kb[pl.ds(at, page_len), :])
                put_v(at, vb[pl.ds(at, page_len), :])

            @pl.when(g >= n_pages)
            def _():
                for h in heads:
                    kh[h, pl.ds(at, page_len), :] = zero
                    vh[h, pl.ds(at, page_len), :] = zero
            return c
        lax.fori_loop(0, n_cb * per, prep_page, 0)

    if prefix:
        for i in range(len(piece)):
            for x in piece_copies(i):
                x.wait()
        total_p = sum(n for _, n in piece)

        def prep_prefix(j, c):
            at = pl.multiple_of(base_p + j * STEP, STEP)
            put_k(at, kb[pl.ds(at, STEP), :])
            put_v(at, vb[pl.ds(at, STEP), :])
            return c
        lax.fori_loop(0, total_p // STEP, prep_prefix, 0)

    def dots(q, h, start, n):
        return lax.dot_general(q, kh[h, pl.ds(start, n), :], (((1,), (1,)), ((), ())), preferred_element_type=f32)

    def fold(state, s, h, start, n):
        top = jnp.max(s, axis=1, keepdims=True)
        new = top if state is None else jnp.maximum(state[0], top)
        p = jnp.exp2((s - new) * SCALE).astype(bf16)
        add = jnp.dot(p, vh[h, pl.ds(start, n), :], preferred_element_type=f32)
        return new, add if state is None else state[1] * jnp.exp2((state[0] - new) * SCALE) + add

    def tile(qt, carry):
        at = pl.multiple_of(qt * bq, bq)
        rows = pl.ds(at, bq)
        qs = [qh[h, rows, :] for h in heads]
        if local:
            seen = lax.broadcasted_iota(jnp.int32, (bq, span), 1) <= lax.broadcasted_iota(jnp.int32, (bq, span), 0) + at
            ss = [dots(q, h, 0, span) for q, h in zip(qs, heads)]
            states = [fold(None, jnp.where(seen, s, NEG), h, 0, span) for s, h in zip(ss, heads)]

            def cache_block(masked, j, sts):
                start = pl.multiple_of(base_c + j * bk, math.gcd(base_c, bk))
                ss = [dots(q, h, start, bk) for q, h in zip(qs, heads)]
                if masked:
                    ok = lax.broadcasted_iota(jnp.int32, (bq, bk), 1) < cached - j * bk
                    ss = [jnp.where(ok, s, NEG) for s in ss]
                return tuple(fold(sx, s, h, start, bk) for sx, s, h in zip(sts, ss, heads))
            states = lax.fori_loop(0, n_full, functools.partial(cache_block, False), tuple(states))
            states = lax.fori_loop(n_full, n_cb, functools.partial(cache_block, True), states)
        else:
            accs = [st[h, rows, :] for h in heads]
            states = [(a[:, TOP:TOP + 1], a) for a in accs]
        if prefix:
            nb = total_p // bk
            for j in range(nb):
                ss = [dots(q, h, base_p + j * bk, bk) for q, h in zip(qs, heads)]
                states = [fold(sx, s, h, base_p + j * bk, bk) for sx, s, h in zip(states, ss, heads)]
            out[rows, :] = jnp.concatenate([(acc / acc[:, SUM:SUM + 1])[:, :HD] for _, acc in states],
                                           axis=1).astype(bf16)
        else:
            lane = lax.broadcasted_iota(jnp.int32, (bq, LANES), 1)
            for h, (m, acc) in zip(heads, states):
                st[h, rows, :] = jnp.where(lane == TOP, m, acc)
        return carry

    lax.fori_loop(0, pl.cdiv(live, bq), tile, 0)


def attend(scal, span, page_len, max_pages, local=None, carry=None, pieces=None, bq=256, bk=1024):
    info, at = [], 0
    for p in pieces or []:
        info.append((at, p.shape[1]))
        at += p.shape[1]
    bq = math.gcd(span, bq)
    bk = math.gcd(bk, at) if pieces else bk
    bk = math.gcd(bk, max_pages * page_len)
    keys = (span + max_pages * page_len if local else 0) + at
    any_ = pl.BlockSpec(memory_space=pl.ANY)
    smem = pl.BlockSpec(memory_space=pltpu.SMEM)
    vmem = pl.BlockSpec(memory_space=pltpu.VMEM)
    heads = jax.ShapeDtypeStruct((GROUP, span, LANES), bf16)
    state = jax.ShapeDtypeStruct((GROUP, span, LANES), f32)
    args, in_specs, outs, scratch = [scal], [smem], [], []
    if local:
        args += list(local)
        in_specs += [any_, any_, vmem]
    else:
        args += list(carry)
        in_specs += [vmem] * 2
    if pieces:
        args += list(pieces)
        in_specs += [any_] * len(pieces)
        outs.append(jax.ShapeDtypeStruct((span, GW), bf16))
    if local:
        if pieces:
            scratch.append(pltpu.VMEM(heads.shape, bf16))
        else:
            outs += [heads, state]
        scratch += [
            pltpu.VMEM((2, span, GW), bf16),
            pltpu.SemaphoreType.DMA((3,)),
            pltpu.SemaphoreType.DMA((2, max_pages)),
        ]
    scratch += [pltpu.VMEM((keys, GW), bf16)] * 2 + [pltpu.VMEM((GROUP, keys, LANES), bf16)] * 2
    if pieces:
        scratch += [pltpu.SemaphoreType.DMA((2, len(pieces)))]
    res = pl.pallas_call(
        functools.partial(attend_kernel, local=bool(local), prefix=bool(pieces), piece=info, span=span, page_len=page_len,
                          max_pages=max_pages, bq=bq, bk=bk),
        out_shape=outs,
        in_specs=in_specs,
        out_specs=[vmem] * len(outs),
        scratch_shapes=scratch,
        compiler_params=pltpu.CompilerParams(vmem_limit_bytes=56 << 20),
        cost_estimate=pl.CostEstimate(flops=8 * span * keys * GROUP * 2 * LANES, bytes_accessed=8 << 20,
                                      transcendentals=span * keys * GROUP),
        name="attend_" + "new" * bool(local) + "prefix" * bool(pieces),
    )(*args)
    return res[0] if pieces else tuple(res)


def project_kernel(scal, *rest, n, bq, depth):
    pieces, w, bias, out, held = rest[:n], rest[n], rest[n + 1], rest[n + 2], rest[n + 3]
    live = scal[0]
    span, cols = out.shape

    @pl.when(pl.program_id(0) == 0)
    def _():
        for i in range(n):
            held[:, pl.ds(pl.multiple_of(scal[1 + i], LANES), depth)] = pieces[i][...]

    for qt in range(span // bq):
        rows = pl.ds(qt * bq, bq)

        @pl.when(qt * bq < live)
        def _():
            acc = jnp.dot(held[rows, :], w[...], preferred_element_type=f32) + bias[...]
            ok = lax.broadcasted_iota(jnp.int32, (bq, cols), 0) + qt * bq < live
            out[rows, :] = jnp.where(ok, acc, 0.0).astype(bf16)

        @pl.when(qt * bq >= live)
        def _():
            out[rows, :] = jnp.zeros((bq, cols), bf16)


def project(live, offsets, pieces, weight, bias):
    span, depth = pieces[0].shape
    k, cols = weight.shape
    bn = math.gcd(cols, 512)
    n = len(pieces)
    scal = jnp.stack([jnp.asarray(x, jnp.int32) for x in [live] + list(offsets)])
    return pl.pallas_call(
        functools.partial(project_kernel, n=n, bq=math.gcd(span, 256), depth=depth),
        grid=(cols // bn,),
        out_shape=jax.ShapeDtypeStruct((span, cols), bf16),
        in_specs=[pl.BlockSpec(memory_space=pltpu.SMEM)]
        + [pl.BlockSpec((span, depth), lambda j: (0, 0), pipeline_mode=pl.Buffered(1))] * n
        + [pl.BlockSpec((k, bn), lambda j: (0, j)), pl.BlockSpec((1, bn), lambda j: (0, j))],
        out_specs=pl.BlockSpec((span, bn), lambda j: (0, j)),
        scratch_shapes=[pltpu.VMEM((span, k), bf16)],
        compiler_params=pltpu.CompilerParams(vmem_limit_bytes=48 << 20),
        cost_estimate=pl.CostEstimate(flops=2 * span * k * cols, bytes_accessed=2 * (k * cols + span * (k + cols)),
                                      transcendentals=0),
        name="project",
    )(scal, *pieces, weight, bias.reshape(1, cols))


def rotary_angles(positions):
    half = ROT // 2
    inv = jnp.power(10000.0, -jnp.arange(half, dtype=f32) * 2.0 / ROT)
    ang = positions.astype(f32)[:, None] * inv[None, :]
    return jnp.concatenate([jnp.cos(ang), jnp.sin(ang)], axis=1)


def chip_ring(chips):
    if chips == 8:
        return [2 * z for z in range(4)] + [2 * z + 1 for z in (3, 2, 1, 0)]
    return list(range(chips))


def after(x, *deps):
    return lax.optimization_barrier((x,) + deps)[0]


def local_fn(qkv, prefix_kv, cache_pool, page_table, cached_lens, span_lens, dense_weight, dense_bias):
    tok, fsdp = lax.axis_size("tok"), lax.axis_size("fsdp")
    span, _, width = qkv.shape
    qkv = jnp.transpose(qkv, (1, 0, 2))
    pool = cache_pool[0]
    max_pages, _, page_len, _ = pool.shape
    prefix_len = prefix_kv.shape[1] * tok
    f = lax.axis_index("fsdp")
    meta = jnp.concatenate([cached_lens, span_lens, page_table[0]])
    rows = jnp.arange(span, dtype=jnp.int32)

    def scalars(m, col, pcol):
        return jnp.concatenate([m[:2], jnp.stack([jnp.asarray(col, jnp.int32), jnp.asarray(pcol, jnp.int32)]), m[2:]])

    if width % (2 * GW) or tok % 2 or fsdp != 2:
        table = rotary_angles(prefix_len + meta[0] + rows)
        whole = lax.all_gather(prefix_kv, "tok", axis=1, tiled=True)
        pieces, offsets = [], []
        for g in range(width // GW):
            got = attend(scalars(meta, g * GW, g * GW), span, page_len, max_pages, local=(qkv, pool, table), pieces=[whole])
            every = lax.all_gather(got, "fsdp", axis=0)
            for i in range(fsdp):
                pieces.append(every[i])
                offsets.append(i * width + g * GW)
        return project(meta[1], offsets, pieces, dense_weight, dense_bias)

    half = width // 2
    c = lax.axis_index("tok") % 2
    swap_pairs = [(i, i ^ 1) for i in range(tok)]
    ring = chip_ring(tok // 2)
    n = len(ring)
    ahead = [(2 * ring[i] + k, 2 * ring[(i + 1) % n] + k) for i in range(n) for k in range(2)]
    back = [(b, a) for a, b in ahead]

    def swap(x):
        return lax.ppermute(x, "tok", swap_pairs)

    def part(x, which):
        return lax.dynamic_slice_in_dim(x, which * half, half, x.ndim - 1)

    meta2 = swap(meta)
    mine = jnp.concatenate([part(prefix_kv, c), swap(part(prefix_kv, 1 - c))], axis=1)
    hop = {1: (lax.ppermute(mine, "tok", ahead), lax.ppermute(mine, "tok", back))}
    qkv2 = swap(after(qkv, mine[0, 0, 0]))
    pool2 = swap(after(pool, mine[0, 0, 0]))
    angles = rotary_angles(prefix_len + meta[0] + rows)
    angles2 = rotary_angles(prefix_len + meta2[0] + rows)
    groups = [g * GW for g in range(half // GW)]
    mates = ((meta, qkv, pool, angles), (meta2, qkv2, pool2, angles2))
    units = [(who, col) for who in (0, 1) for col in groups]
    steps = n // 2
    carries, gate = {}, []
    for i, (who, col) in enumerate(units):
        m, a, b, t = mates[who]
        carries[who, col] = attend(after(scalars(m, c * half + col, col), *gate), span, page_len, max_pages, local=(a, b, t))
        d = i + 2
        if d <= steps:
            fw, bw = hop[d - 1]
            gate = [fw[0, 0, 0], bw[0, 0, 0]]
            if d == steps:
                k = fw.shape[1] // 2
                fw, bw = fw[:, :k], bw[:, k:]
            hop[d] = (lax.ppermute(fw, "tok", ahead), lax.ppermute(bw, "tok", back))
        else:
            gate = []
    pieces = [mine] + [x for d in range(1, steps + 1) for x in hop[d]]
    ypairs = [(0, 1), (1, 0)]
    proj, offsets, last = [], [], None
    for who, col in [(w, col) for w in (1, 0) for col in groups]:
        s = scalars(mates[who][0], 0, col)
        s = s if last is None else after(s, last[0, 0])
        got = attend(s, span, page_len, max_pages, carry=carries[who, col], pieces=pieces)
        last = got
        far = lax.ppermute(got, "fsdp", ypairs)
        if who:
            got, far = swap(got), swap(far)
        at = (1 - c if who else c) * half + col
        proj += [got, far]
        offsets += [f * width + at, (1 - f) * width + at]
    return project(meta[1], offsets, proj, dense_weight, dense_bias)


def solution(mesh):
    return jax.shard_map(
        local_fn,
        mesh=mesh,
        in_specs=(
            P("tok", None, "fsdp"),
            P(None, "tok", "fsdp"),
            P("tok", None, None, None, "fsdp"),
            P("tok", None),
            P("tok"),
            P("tok"),
            P(None, "fsdp"),
            P("fsdp"),
        ),
        out_specs=P("tok", "fsdp"),
        check_vma=False,
    )
```

```python
import functools
import math

import jax
import jax.numpy as jnp
from jax import lax
from jax.experimental import pallas as pl
from jax.experimental.pallas import tpu as pltpu
from jax.sharding import PartitionSpec as P

HD = 96
ROT = 24
LANES = 128
GROUP = 4
GW = GROUP * HD
NEG = -1e30
f32, bf16 = jnp.float32, jnp.bfloat16
SCALE = HD ** -0.5 * math.log2(math.e)
SUM, TOP = HD, HD + 1
STEP = 128


def realign(x, h):
    lo = h * HD
    first = lo // LANES * LANES
    off = lo - first
    if off == 0:
        return x[:, first:first + LANES]
    if off + HD <= LANES:
        return pltpu.roll(x[:, first:first + LANES], LANES - off, 1)
    return pltpu.roll(x[:, first:first + 2 * LANES], 2 * LANES - off, 1)[:, :LANES]


def turn_tables(angles):
    half = ROT // 2
    row = lax.broadcasted_iota(jnp.int32, (ROT, LANES), 0)
    lane = lax.broadcasted_iota(jnp.int32, (ROT, LANES), 1)

    def pick(where_, sign=1.0):
        return jnp.dot(angles, jnp.where(where_, sign, 0.0), precision=lax.Precision.HIGHEST,
                       preferred_element_type=f32)
    here = pick((lane == row) & (row < half) | (lane == row + half) & (row < half))
    rest = lax.broadcasted_iota(jnp.int32, here.shape, 1) >= ROT
    return (jnp.where(rest, 1.0, here), pick((lane == row - half) & (row >= half), -1.0),
            pick((lane == row) & (row >= half)))


def attend_kernel(scal, *rest, local, prefix, piece, span, page_len, max_pages, bq, bk):
    it = iter(rest)
    if local:
        qkv, pool, angles = next(it), next(it), next(it)
    else:
        qh, st = next(it), next(it)
    pieces = [next(it) for _ in piece] if prefix else []
    if prefix:
        out = next(it)
    if local:
        qh = next(it)
        if not prefix:
            st = next(it)
        qk, sem_q, sem_c = next(it), next(it), next(it)
    kb, vb, kh, vh = next(it), next(it), next(it), next(it)
    if prefix:
        sem_p = next(it)
    cached = scal[0]
    live = scal[1]
    cols = pl.ds(pl.multiple_of(scal[2], LANES), GW)
    pcol = pl.ds(pl.multiple_of(scal[3], LANES), GW)
    n_pages = pl.cdiv(cached, page_len)
    base_c = span if local else 0
    base_p = span + max_pages * page_len if local else 0
    per = bk // page_len
    n_cb = pl.cdiv(cached, bk)
    n_full = cached // bk
    heads = range(GROUP)
    zero = jnp.zeros((STEP, LANES), bf16)

    def put_v(at, v):
        lane = lax.broadcasted_iota(jnp.int32, (STEP, LANES), 1)
        one = jnp.where(lane == SUM, 1.0, 0.0).astype(bf16)
        for h in heads:
            vh[h, pl.ds(at, STEP), :] = jnp.where(lane < HD, realign(v, h), one)

    def put_k(at, k):
        for h in heads:
            kh[h, pl.ds(at, STEP), :] = realign(k, h)

    if local:
        new_copies = [
            pltpu.make_async_copy(qkv.at[0, :, cols], qk.at[0], sem_q.at[0]),
            pltpu.make_async_copy(qkv.at[1, :, cols], qk.at[1], sem_q.at[1]),
            pltpu.make_async_copy(qkv.at[2, :, cols], vb.at[pl.ds(0, span), :], sem_q.at[2]),
        ]
        for c in new_copies:
            c.start()

        def page_copies(g):
            dst = pl.ds(pl.multiple_of(base_c + g * page_len, page_len), page_len)
            return (pltpu.make_async_copy(pool.at[scal[4 + g], 0, :, cols], kb.at[dst, :], sem_c.at[0, g]),
                    pltpu.make_async_copy(pool.at[scal[4 + g], 1, :, cols], vb.at[dst, :], sem_c.at[1, g]))

        def start_page(g, c):
            for x in page_copies(g):
                x.start()
            return c
        lax.fori_loop(0, n_pages, start_page, 0)

    def piece_copies(i):
        at, n = piece[i]
        dst = pl.ds(base_p + at, n)
        return (pltpu.make_async_copy(pieces[i].at[0, :, pcol], kb.at[dst, :], sem_p.at[0, i]),
                pltpu.make_async_copy(pieces[i].at[1, :, pcol], vb.at[dst, :], sem_p.at[1, i]))

    if prefix:
        for i in range(len(piece)):
            for x in piece_copies(i):
                x.start()

    if local:
        for c in new_copies:
            c.wait()

        def prep_new(j, c):
            at = pl.multiple_of(j * STEP, STEP)
            r = pl.ds(at, STEP)
            lane = lax.broadcasted_iota(jnp.int32, (STEP, LANES), 1)
            ta, tb, tc = turn_tables(angles[r, :])

            def turn(x, h):
                x = realign(x, h).astype(f32)
                x = x * ta + pltpu.roll(x, LANES - ROT // 2, 1) * tb + pltpu.roll(x, ROT // 2, 1) * tc
                return jnp.where(lane < HD, x, 0.0).astype(bf16)
            q, k = qk[0, r, :], qk[1, r, :]
            for h in heads:
                qh[h, r, :] = turn(q, h)
                kh[h, r, :] = turn(k, h)
            put_v(at, vb[r, :])
            return c
        lax.fori_loop(0, span // STEP, prep_new, 0)

        def prep_page(g, c):
            at = pl.multiple_of(base_c + g * page_len, page_len)

            @pl.when(g < n_pages)
            def _():
                for x in page_copies(g):
                    x.wait()
                put_k(at, kb[pl.ds(at, page_len), :])
                put_v(at, vb[pl.ds(at, page_len), :])

            @pl.when(g >= n_pages)
            def _():
                for h in heads:
                    kh[h, pl.ds(at, page_len), :] = zero
                    vh[h, pl.ds(at, page_len), :] = zero
            return c
        lax.fori_loop(0, n_cb * per, prep_page, 0)

    if prefix:
        for i in range(len(piece)):
            for x in piece_copies(i):
                x.wait()
        total_p = sum(n for _, n in piece)

        def prep_prefix(j, c):
            at = pl.multiple_of(base_p + j * STEP, STEP)
            put_k(at, kb[pl.ds(at, STEP), :])
            put_v(at, vb[pl.ds(at, STEP), :])
            return c
        lax.fori_loop(0, total_p // STEP, prep_prefix, 0)

    def dots(q, h, start, n):
        return lax.dot_general(q, kh[h, pl.ds(start, n), :], (((1,), (1,)), ((), ())), preferred_element_type=f32)

    def fold(state, s, h, start, n):
        top = jnp.max(s, axis=1, keepdims=True)
        new = top if state is None else jnp.maximum(state[0], top)
        p = jnp.exp2((s - new) * SCALE).astype(bf16)
        add = jnp.dot(p, vh[h, pl.ds(start, n), :], preferred_element_type=f32)
        return new, add if state is None else state[1] * jnp.exp2((state[0] - new) * SCALE) + add

    def tile(qt, carry):
        at = pl.multiple_of(qt * bq, bq)
        rows = pl.ds(at, bq)
        qs = [qh[h, rows, :] for h in heads]
        if local:
            seen = lax.broadcasted_iota(jnp.int32, (bq, span), 1) <= lax.broadcasted_iota(jnp.int32, (bq, span), 0) + at
            ss = [dots(q, h, 0, span) for q, h in zip(qs, heads)]
            states = [fold(None, jnp.where(seen, s, NEG), h, 0, span) for s, h in zip(ss, heads)]

            def cache_block(masked, j, sts):
                start = pl.multiple_of(base_c + j * bk, math.gcd(base_c, bk))
                ss = [dots(q, h, start, bk) for q, h in zip(qs, heads)]
                if masked:
                    ok = lax.broadcasted_iota(jnp.int32, (bq, bk), 1) < cached - j * bk
                    ss = [jnp.where(ok, s, NEG) for s in ss]
                return tuple(fold(sx, s, h, start, bk) for sx, s, h in zip(sts, ss, heads))
            states = lax.fori_loop(0, n_full, functools.partial(cache_block, False), tuple(states))
            states = lax.fori_loop(n_full, n_cb, functools.partial(cache_block, True), states)
        else:
            accs = [st[h, rows, :] for h in heads]
            states = [(a[:, TOP:TOP + 1], a) for a in accs]
        if prefix:
            nb = total_p // bk
            for j in range(nb):
                ss = [dots(q, h, base_p + j * bk, bk) for q, h in zip(qs, heads)]
                states = [fold(sx, s, h, base_p + j * bk, bk) for sx, s, h in zip(states, ss, heads)]
            out[rows, :] = jnp.concatenate([(acc / acc[:, SUM:SUM + 1])[:, :HD] for _, acc in states],
                                           axis=1).astype(bf16)
        else:
            lane = lax.broadcasted_iota(jnp.int32, (bq, LANES), 1)
            for h, (m, acc) in zip(heads, states):
                st[h, rows, :] = jnp.where(lane == TOP, m, acc)
        return carry

    lax.fori_loop(0, pl.cdiv(live, bq), tile, 0)


def attend(scal, span, page_len, max_pages, local=None, carry=None, pieces=None, bq=256, bk=1024):
    info, at = [], 0
    for p in pieces or []:
        info.append((at, p.shape[1]))
        at += p.shape[1]
    bq = math.gcd(span, bq)
    bk = math.gcd(bk, at) if pieces else bk
    bk = math.gcd(bk, max_pages * page_len)
    keys = (span + max_pages * page_len if local else 0) + at
    any_ = pl.BlockSpec(memory_space=pl.ANY)
    smem = pl.BlockSpec(memory_space=pltpu.SMEM)
    vmem = pl.BlockSpec(memory_space=pltpu.VMEM)
    heads = jax.ShapeDtypeStruct((GROUP, span, LANES), bf16)
    state = jax.ShapeDtypeStruct((GROUP, span, LANES), f32)
    args, in_specs, outs, scratch = [scal], [smem], [], []
    if local:
        args += list(local)
        in_specs += [any_, any_, vmem]
    else:
        args += list(carry)
        in_specs += [vmem] * 2
    if pieces:
        args += list(pieces)
        in_specs += [any_] * len(pieces)
        outs.append(jax.ShapeDtypeStruct((span, GW), bf16))
    if local:
        if pieces:
            scratch.append(pltpu.VMEM(heads.shape, bf16))
        else:
            outs += [heads, state]
        scratch += [
            pltpu.VMEM((2, span, GW), bf16),
            pltpu.SemaphoreType.DMA((3,)),
            pltpu.SemaphoreType.DMA((2, max_pages)),
        ]
    scratch += [pltpu.VMEM((keys, GW), bf16)] * 2 + [pltpu.VMEM((GROUP, keys, LANES), bf16)] * 2
    if pieces:
        scratch += [pltpu.SemaphoreType.DMA((2, len(pieces)))]
    res = pl.pallas_call(
        functools.partial(attend_kernel, local=bool(local), prefix=bool(pieces), piece=info, span=span, page_len=page_len,
                          max_pages=max_pages, bq=bq, bk=bk),
        out_shape=outs,
        in_specs=in_specs,
        out_specs=[vmem] * len(outs),
        scratch_shapes=scratch,
        compiler_params=pltpu.CompilerParams(vmem_limit_bytes=56 << 20),
        cost_estimate=pl.CostEstimate(flops=8 * span * keys * GROUP * 2 * LANES, bytes_accessed=8 << 20,
                                      transcendentals=span * keys * GROUP),
        name="attend_" + "new" * bool(local) + "prefix" * bool(pieces),
    )(*args)
    return res[0] if pieces else tuple(res)


def project_kernel(scal, *rest, n, bq, depth):
    pieces, w, bias, out, held = rest[:n], rest[n], rest[n + 1], rest[n + 2], rest[n + 3]
    live = scal[0]
    span, cols = out.shape

    @pl.when(pl.program_id(0) == 0)
    def _():
        for i in range(n):
            held[:, pl.ds(pl.multiple_of(scal[1 + i], LANES), depth)] = pieces[i][...]

    for qt in range(span // bq):
        rows = pl.ds(qt * bq, bq)

        @pl.when(qt * bq < live)
        def _():
            acc = jnp.dot(held[rows, :], w[...], preferred_element_type=f32) + bias[...]
            ok = lax.broadcasted_iota(jnp.int32, (bq, cols), 0) + qt * bq < live
            out[rows, :] = jnp.where(ok, acc, 0.0).astype(bf16)

        @pl.when(qt * bq >= live)
        def _():
            out[rows, :] = jnp.zeros((bq, cols), bf16)


def project(live, offsets, pieces, weight, bias):
    span, depth = pieces[0].shape
    k, cols = weight.shape
    bn = math.gcd(cols, 512)
    n = len(pieces)
    scal = jnp.stack([jnp.asarray(x, jnp.int32) for x in [live] + list(offsets)])
    return pl.pallas_call(
        functools.partial(project_kernel, n=n, bq=math.gcd(span, 256), depth=depth),
        grid=(cols // bn,),
        out_shape=jax.ShapeDtypeStruct((span, cols), bf16),
        in_specs=[pl.BlockSpec(memory_space=pltpu.SMEM)]
        + [pl.BlockSpec((span, depth), lambda j: (0, 0), pipeline_mode=pl.Buffered(1))] * n
        + [pl.BlockSpec((k, bn), lambda j: (0, j)), pl.BlockSpec((1, bn), lambda j: (0, j))],
        out_specs=pl.BlockSpec((span, bn), lambda j: (0, j)),
        scratch_shapes=[pltpu.VMEM((span, k), bf16)],
        compiler_params=pltpu.CompilerParams(vmem_limit_bytes=48 << 20),
        cost_estimate=pl.CostEstimate(flops=2 * span * k * cols, bytes_accessed=2 * (k * cols + span * (k + cols)),
                                      transcendentals=0),
        name="project",
    )(scal, *pieces, weight, bias.reshape(1, cols))


def rotary_angles(positions):
    half = ROT // 2
    inv = jnp.power(10000.0, -jnp.arange(half, dtype=f32) * 2.0 / ROT)
    ang = positions.astype(f32)[:, None] * inv[None, :]
    return jnp.concatenate([jnp.cos(ang), jnp.sin(ang)], axis=1)


def chip_ring(chips):
    if chips == 8:
        return [2 * z for z in range(4)] + [2 * z + 1 for z in (3, 2, 1, 0)]
    return list(range(chips))


def after(x, *deps):
    return lax.optimization_barrier((x,) + deps)[0]


def local_fn(qkv, prefix_kv, cache_pool, page_table, cached_lens, span_lens, dense_weight, dense_bias):
    tok, fsdp = lax.axis_size("tok"), lax.axis_size("fsdp")
    span, _, width = qkv.shape
    qkv = jnp.transpose(qkv, (1, 0, 2))
    pool = cache_pool[0]
    max_pages, _, page_len, _ = pool.shape
    prefix_len = prefix_kv.shape[1] * tok
    f = lax.axis_index("fsdp")
    meta = jnp.concatenate([cached_lens, span_lens, page_table[0]])
    rows = jnp.arange(span, dtype=jnp.int32)

    def scalars(m, col, pcol):
        return jnp.concatenate([m[:2], jnp.stack([jnp.asarray(col, jnp.int32), jnp.asarray(pcol, jnp.int32)]), m[2:]])

    if width % (2 * GW) or tok % 2 or fsdp != 2:
        table = rotary_angles(prefix_len + meta[0] + rows)
        whole = lax.all_gather(prefix_kv, "tok", axis=1, tiled=True)
        pieces, offsets = [], []
        for g in range(width // GW):
            got = attend(scalars(meta, g * GW, g * GW), span, page_len, max_pages, local=(qkv, pool, table), pieces=[whole])
            every = lax.all_gather(got, "fsdp", axis=0)
            for i in range(fsdp):
                pieces.append(every[i])
                offsets.append(i * width + g * GW)
        return project(meta[1], offsets, pieces, dense_weight, dense_bias)

    half = width // 2
    c = lax.axis_index("tok") % 2
    swap_pairs = [(i, i ^ 1) for i in range(tok)]
    ring = chip_ring(tok // 2)
    n = len(ring)
    ahead = [(2 * ring[i] + k, 2 * ring[(i + 1) % n] + k) for i in range(n) for k in range(2)]
    back = [(b, a) for a, b in ahead]

    def swap(x):
        return lax.ppermute(x, "tok", swap_pairs)

    def part(x, which):
        return lax.dynamic_slice_in_dim(x, which * half, half, x.ndim - 1)

    meta2 = swap(meta)
    mine = jnp.concatenate([part(prefix_kv, c), swap(part(prefix_kv, 1 - c))], axis=1)
    hop = {1: (lax.ppermute(mine, "tok", ahead), lax.ppermute(mine, "tok", back))}
    qkv2 = swap(after(qkv, mine[0, 0, 0]))
    pool2 = swap(after(pool, mine[0, 0, 0]))
    angles = rotary_angles(prefix_len + meta[0] + rows)
    angles2 = rotary_angles(prefix_len + meta2[0] + rows)
    groups = [g * GW for g in range(half // GW)]
    mates = ((meta, qkv, pool, angles), (meta2, qkv2, pool2, angles2))
    units = [(who, col) for who in (0, 1) for col in groups]
    steps = n // 2
    carries, gate = {}, []
    for i, (who, col) in enumerate(units):
        m, a, b, t = mates[who]
        carries[who, col] = attend(after(scalars(m, c * half + col, col), *gate), span, page_len, max_pages, local=(a, b, t))
        d = i + 2
        if d <= steps:
            fw, bw = hop[d - 1]
            gate = [fw[0, 0, 0], bw[0, 0, 0]]
            if d == steps:
                k = fw.shape[1] // 2
                fw, bw = fw[:, :k], bw[:, k:]
            fw, bw, carries[who, col] = lax.optimization_barrier((fw, bw, carries[who, col]))
            hop[d] = (lax.ppermute(fw, "tok", ahead), lax.ppermute(bw, "tok", back))
        else:
            gate = []
    pieces = [mine] + [x for d in range(1, steps + 1) for x in hop[d]]
    ypairs = [(0, 1), (1, 0)]
    proj, offsets, last = [], [], None
    for who, col in [(w, col) for w in (1, 0) for col in groups]:
        s = scalars(mates[who][0], 0, col)
        s = s if last is None else after(s, last[0, 0])
        got = attend(s, span, page_len, max_pages, carry=carries[who, col], pieces=pieces)
        last = got
        far = lax.ppermute(got, "fsdp", ypairs)
        if who:
            got, far = swap(got), swap(far)
        at = (1 - c if who else c) * half + col
        proj += [got, far]
        offsets += [f * width + at, (1 - f) * width + at]
    return project(meta[1], offsets, proj, dense_weight, dense_bias)


def solution(mesh):
    return jax.shard_map(
        local_fn,
        mesh=mesh,
        in_specs=(
            P("tok", None, "fsdp"),
            P(None, "tok", "fsdp"),
            P("tok", None, None, None, "fsdp"),
            P("tok", None),
            P("tok"),
            P("tok"),
            P(None, "fsdp"),
            P("fsdp"),
        ),
        out_specs=P("tok", "fsdp"),
        check_vma=False,
    )
```

```python
import functools
import math

import jax
import jax.numpy as jnp
from jax import lax
from jax.experimental import pallas as pl
from jax.experimental.pallas import tpu as pltpu
from jax.sharding import PartitionSpec as P

HD = 96
ROT = 24
LANES = 128
GROUP = 4
GW = GROUP * HD
NEG = -1e30
f32, bf16 = jnp.float32, jnp.bfloat16
SCALE = HD ** -0.5 * math.log2(math.e)
SUM, TOP = HD, HD + 1
STEP = 128
HEAD = 5


def realign(x, h):
    lo = h * HD
    first = lo // LANES * LANES
    off = lo - first
    if off == 0:
        return x[:, first:first + LANES]
    if off + HD <= LANES:
        return pltpu.roll(x[:, first:first + LANES], LANES - off, 1)
    return pltpu.roll(x[:, first:first + 2 * LANES], 2 * LANES - off, 1)[:, :LANES]


def attend_kernel(scal, *rest, local, prefix, send, piece, span, page_len, max_pages, bq, bk):
    it = iter(rest)
    if local:
        qkv, pool, angles = next(it), next(it), next(it)
    else:
        qh, st = next(it), next(it)
    pieces = [next(it) for _ in piece] if prefix else []
    if prefix:
        out = next(it)
    if local:
        qh = next(it)
        if not prefix:
            st = next(it)
        if send:
            qkv_out, pool_out = next(it), next(it)
        qk, sem_q, sem_c = next(it), next(it), next(it)
        if send:
            sem_s, sem_t = next(it), next(it)
    kb, vb, kh, vh = next(it), next(it), next(it), next(it)
    if prefix:
        sem_p = next(it)
    cached = scal[0]
    live = scal[1]
    cols = pl.ds(pl.multiple_of(scal[2], LANES), GW)
    pcol = pl.ds(pl.multiple_of(scal[3], LANES), GW)
    n_pages = pl.cdiv(cached, page_len)
    base_c = span if local else 0
    base_p = span + max_pages * page_len if local else 0
    per = bk // page_len
    n_cb = pl.cdiv(cached, bk)
    n_full = cached // bk
    heads = range(GROUP)
    zero = jnp.zeros((STEP, LANES), bf16)

    def put_v(at, v):
        lane = lax.broadcasted_iota(jnp.int32, (STEP, LANES), 1)
        one = jnp.where(lane == SUM, 1.0, 0.0).astype(bf16)
        for h in heads:
            vh[h, pl.ds(at, STEP), :] = jnp.where(lane < HD, realign(v, h), one)

    def put_k(at, k):
        for h in heads:
            kh[h, pl.ds(at, STEP), :] = realign(k, h)

    if local:
        new_copies = [
            pltpu.make_async_copy(qkv.at[0, :, cols], qk.at[0], sem_q.at[0]),
            pltpu.make_async_copy(qkv.at[1, :, cols], qk.at[1], sem_q.at[1]),
            pltpu.make_async_copy(qkv.at[2, :, cols], vb.at[pl.ds(0, span), :], sem_q.at[2]),
        ]
        for c in new_copies:
            c.start()

        def page_copies(g):
            dst = pl.ds(pl.multiple_of(base_c + g * page_len, page_len), page_len)
            return (pltpu.make_async_copy(pool.at[scal[HEAD + g], 0, :, cols], kb.at[dst, :], sem_c.at[0, g]),
                    pltpu.make_async_copy(pool.at[scal[HEAD + g], 1, :, cols], vb.at[dst, :], sem_c.at[1, g]))

        def start_page(g, c):
            for x in page_copies(g):
                x.start()
            return c
        lax.fori_loop(0, n_pages, start_page, 0)

        if send:
            scol = pl.ds(pl.multiple_of(scal[4], LANES), qkv_out.shape[2])
            qkv_send = pltpu.make_async_copy(qkv.at[:, :, scol], qkv_out, sem_s)
            qkv_send.start()

            def page_send(g):
                page = scal[HEAD + g]
                return pltpu.make_async_copy(pool.at[page, :, :, scol], pool_out.at[page], sem_t.at[g])

            def start_send(g, c):
                page_send(g).start()
                return c
            lax.fori_loop(0, n_pages, start_send, 0)

    def piece_copies(i):
        at, n = piece[i]
        dst = pl.ds(base_p + at, n)
        return (pltpu.make_async_copy(pieces[i].at[0, :, pcol], kb.at[dst, :], sem_p.at[0, i]),
                pltpu.make_async_copy(pieces[i].at[1, :, pcol], vb.at[dst, :], sem_p.at[1, i]))

    if prefix:
        for i in range(len(piece)):
            for x in piece_copies(i):
                x.start()

    if local:
        for c in new_copies:
            c.wait()

        def prep_new(j, c):
            at = pl.multiple_of(j * STEP, STEP)
            r = pl.ds(at, STEP)
            lane = lax.broadcasted_iota(jnp.int32, (STEP, LANES), 1)
            cosine, sine = angles[0, r, :], angles[1, r, :]

            def turn(x, h):
                x = realign(x, h).astype(f32)
                mate = jnp.where(lane < ROT // 2, pltpu.roll(x, LANES - ROT // 2, 1), pltpu.roll(x, ROT // 2, 1))
                x = x * cosine + mate * sine
                return jnp.where(lane < HD, x, 0.0).astype(bf16)
            q, k = qk[0, r, :], qk[1, r, :]
            for h in heads:
                qh[h, r, :] = turn(q, h)
                kh[h, r, :] = turn(k, h)
            put_v(at, vb[r, :])
            return c
        n_new = pl.cdiv(live, STEP)
        lax.fori_loop(0, n_new, prep_new, 0)

        def clear_new(j, c):
            r = pl.ds(pl.multiple_of(j * STEP, STEP), STEP)
            for h in heads:
                vh[h, r, :] = zero
            return c
        lax.fori_loop(n_new, span // STEP, clear_new, 0)

        def prep_page(g, c):
            at = pl.multiple_of(base_c + g * page_len, page_len)

            @pl.when(g < n_pages)
            def _():
                for x in page_copies(g):
                    x.wait()
                put_k(at, kb[pl.ds(at, page_len), :])
                put_v(at, vb[pl.ds(at, page_len), :])

            @pl.when(g >= n_pages)
            def _():
                for h in heads:
                    kh[h, pl.ds(at, page_len), :] = zero
                    vh[h, pl.ds(at, page_len), :] = zero
            return c
        lax.fori_loop(0, n_cb * per, prep_page, 0)

    if prefix:
        for i in range(len(piece)):
            for x in piece_copies(i):
                x.wait()
        total_p = sum(n for _, n in piece)

        def prep_prefix(j, c):
            at = pl.multiple_of(base_p + j * STEP, STEP)
            put_k(at, kb[pl.ds(at, STEP), :])
            put_v(at, vb[pl.ds(at, STEP), :])
            return c
        lax.fori_loop(0, total_p // STEP, prep_prefix, 0)

    def dots(q, h, start, n):
        return lax.dot_general(q, kh[h, pl.ds(start, n), :], (((1,), (1,)), ((), ())), preferred_element_type=f32)

    def fold(state, s, h, start, n):
        top = jnp.max(s, axis=1, keepdims=True)
        new = top if state is None else jnp.maximum(state[0], top)
        p = jnp.exp2((s - new) * SCALE).astype(bf16)
        add = jnp.dot(p, vh[h, pl.ds(start, n), :], preferred_element_type=f32)
        return new, add if state is None else state[1] * jnp.exp2((state[0] - new) * SCALE) + add

    def tile(qt, carry):
        at = pl.multiple_of(qt * bq, bq)
        rows = pl.ds(at, bq)
        qs = [qh[h, rows, :] for h in heads]
        if local:
            seen = lax.broadcasted_iota(jnp.int32, (bq, span), 1) <= lax.broadcasted_iota(jnp.int32, (bq, span), 0) + at
            ss = [dots(q, h, 0, span) for q, h in zip(qs, heads)]
            states = [fold(None, jnp.where(seen, s, NEG), h, 0, span) for s, h in zip(ss, heads)]

            def cache_block(masked, j, sts):
                start = pl.multiple_of(base_c + j * bk, math.gcd(base_c, bk))
                ss = [dots(q, h, start, bk) for q, h in zip(qs, heads)]
                if masked:
                    ok = lax.broadcasted_iota(jnp.int32, (bq, bk), 1) < cached - j * bk
                    ss = [jnp.where(ok, s, NEG) for s in ss]
                return tuple(fold(sx, s, h, start, bk) for sx, s, h in zip(sts, ss, heads))
            states = lax.fori_loop(0, n_full, functools.partial(cache_block, False), tuple(states))
            states = lax.fori_loop(n_full, n_cb, functools.partial(cache_block, True), states)
        else:
            accs = [st[h, rows, :] for h in heads]
            states = [(a[:, TOP:TOP + 1], a) for a in accs]
        if prefix:
            nb = total_p // bk
            for j in range(nb):
                ss = [dots(q, h, base_p + j * bk, bk) for q, h in zip(qs, heads)]
                states = [fold(sx, s, h, base_p + j * bk, bk) for sx, s, h in zip(states, ss, heads)]
            out[rows, :] = jnp.concatenate([(acc / acc[:, SUM:SUM + 1])[:, :HD] for _, acc in states],
                                           axis=1).astype(bf16)
        else:
            lane = lax.broadcasted_iota(jnp.int32, (bq, LANES), 1)
            for h, (m, acc) in zip(heads, states):
                st[h, rows, :] = jnp.where(lane == TOP, m, acc)
        return carry

    lax.fori_loop(0, pl.cdiv(live, bq), tile, 0)

    if send:
        def wait_send(g, c):
            page_send(g).wait()
            return c
        qkv_send.wait()
        lax.fori_loop(0, n_pages, wait_send, 0)


def attend(scal, span, page_len, max_pages, local=None, carry=None, pieces=None, send=0, bq=256):
    info, at = [], 0
    for p in pieces or []:
        info.append((at, p.shape[1]))
        at += p.shape[1]
    bq = math.gcd(span, bq)
    bk = math.gcd(1024, max_pages * page_len) if local else math.gcd(2048, at)
    if local and pieces:
        bk = math.gcd(bk, at)
    keys = (span + max_pages * page_len if local else 0) + at
    any_ = pl.BlockSpec(memory_space=pltpu.HBM)
    smem = pl.BlockSpec(memory_space=pltpu.SMEM)
    vmem = pl.BlockSpec(memory_space=pltpu.VMEM)
    heads = jax.ShapeDtypeStruct((GROUP, span, LANES), bf16)
    state = jax.ShapeDtypeStruct((GROUP, span, LANES), f32)
    args, in_specs, outs, scratch = [scal], [smem], [], []
    if local:
        args += list(local)
        in_specs += [any_, any_, vmem]
    else:
        args += list(carry)
        in_specs += [vmem] * 2
    if pieces:
        args += list(pieces)
        in_specs += [any_] * len(pieces)
        outs.append(jax.ShapeDtypeStruct((span, GW), bf16))
    if local:
        if pieces:
            scratch.append(pltpu.VMEM(heads.shape, bf16))
        else:
            outs += [heads, state]
            if send:
                outs += [jax.ShapeDtypeStruct((3, span, send), bf16),
                         jax.ShapeDtypeStruct((max_pages, 2, page_len, send), bf16)]
        scratch += [
            pltpu.VMEM((2, span, GW), bf16),
            pltpu.SemaphoreType.DMA((3,)),
            pltpu.SemaphoreType.DMA((2, max_pages)),
        ]
        if send:
            scratch += [pltpu.SemaphoreType.DMA, pltpu.SemaphoreType.DMA((max_pages,))]
    scratch += [pltpu.VMEM((keys, GW), bf16)] * 2 + [pltpu.VMEM((GROUP, keys, LANES), bf16)] * 2
    if pieces:
        scratch += [pltpu.SemaphoreType.DMA((2, len(pieces)))]
    res = pl.pallas_call(
        functools.partial(attend_kernel, local=bool(local), prefix=bool(pieces), send=bool(send), piece=info, span=span, page_len=page_len,
                          max_pages=max_pages, bq=bq, bk=bk),
        out_shape=outs,
        in_specs=in_specs,
        out_specs=[vmem] * (len(outs) - 2 * bool(send)) + [any_] * (2 * bool(send)),
        scratch_shapes=scratch,
        compiler_params=pltpu.CompilerParams(vmem_limit_bytes=56 << 20),
        cost_estimate=pl.CostEstimate(flops=8 * span * keys * GROUP * 2 * LANES, bytes_accessed=8 << 20,
                                      transcendentals=span * keys * GROUP),
        name="attend_" + "new" * bool(local) + "prefix" * bool(pieces),
    )(*args)
    return res[0] if pieces else tuple(res)


def project_kernel(scal, *rest, n, bq, depth):
    pieces, w, bias, out, held = rest[:n], rest[n], rest[n + 1], rest[n + 2], rest[n + 3]
    live = scal[0]
    span, cols = out.shape

    @pl.when(pl.program_id(0) == 0)
    def _():
        for i in range(n):
            held[:, pl.ds(pl.multiple_of(scal[1 + i], LANES), depth)] = pieces[i][...]

    for k in range(1, span // bq + 1):
        @pl.when(pl.cdiv(live, bq) == k)
        def _():
            acc = jnp.dot(held[0:k * bq, :], w[...], preferred_element_type=f32) + bias[...]
            ok = lax.broadcasted_iota(jnp.int32, acc.shape, 0) < live
            out[0:k * bq, :] = jnp.where(ok, acc, 0.0).astype(bf16)
            if k * bq < span:
                out[k * bq:span, :] = jnp.zeros((span - k * bq, cols), bf16)


def project(live, offsets, pieces, weight, bias):
    span, depth = pieces[0].shape
    k, cols = weight.shape
    bn = math.gcd(cols, 512)
    n = len(pieces)
    scal = jnp.stack([jnp.asarray(x, jnp.int32) for x in [live] + list(offsets)])
    return pl.pallas_call(
        functools.partial(project_kernel, n=n, bq=math.gcd(span, 256), depth=depth),
        grid=(cols // bn,),
        out_shape=jax.ShapeDtypeStruct((span, cols), bf16),
        in_specs=[pl.BlockSpec(memory_space=pltpu.SMEM)]
        + [pl.BlockSpec((span, depth), lambda j: (0, 0), pipeline_mode=pl.Buffered(1))] * n
        + [pl.BlockSpec((k, bn), lambda j: (0, j)), pl.BlockSpec((1, bn), lambda j: (0, j))],
        out_specs=pl.BlockSpec((span, bn), lambda j: (0, j)),
        scratch_shapes=[pltpu.VMEM((span, k), bf16)],
        compiler_params=pltpu.CompilerParams(vmem_limit_bytes=48 << 20),
        cost_estimate=pl.CostEstimate(flops=2 * span * k * cols, bytes_accessed=2 * (k * cols + span * (k + cols)),
                                      transcendentals=0),
        name="project",
    )(scal, *pieces, weight, bias.reshape(1, cols))


def rotary_angles(positions):
    half = ROT // 2
    inv = jnp.power(10000.0, -jnp.arange(half, dtype=f32) * 2.0 / ROT)
    inv = jnp.concatenate([inv, inv, jnp.zeros(LANES - ROT, f32)])
    ang = positions.astype(f32)[:, None] * inv[None, :]
    sign = jnp.where(jnp.arange(LANES) < half, -1.0, 1.0)
    return jnp.stack([jnp.cos(ang), jnp.sin(ang) * sign])


def chip_ring(chips):
    if chips == 8:
        return [2 * z for z in range(4)] + [2 * z + 1 for z in (3, 2, 1, 0)]
    return list(range(chips))


def order(scal, *firsts):
    for x in firsts:
        scal = scal + (x[(slice(0, 1),) * x.ndim].reshape(()).astype(f32) > 1e30).astype(jnp.int32)
    return scal


def local_fn(qkv, prefix_kv, cache_pool, page_table, cached_lens, span_lens, dense_weight, dense_bias):
    tok, fsdp = lax.axis_size("tok"), lax.axis_size("fsdp")
    span, _, width = qkv.shape
    qkv = jnp.transpose(qkv, (1, 0, 2))
    pool = cache_pool[0]
    max_pages, _, page_len, _ = pool.shape
    prefix_len = prefix_kv.shape[1] * tok
    f = lax.axis_index("fsdp")
    meta = jnp.concatenate([cached_lens, span_lens, page_table[0]])
    rows = jnp.arange(span, dtype=jnp.int32)

    def scalars(m, col, pcol, scol=0):
        return jnp.concatenate([m[:2], jnp.stack([jnp.asarray(x, jnp.int32) for x in (col, pcol, scol)]), m[2:]])

    if width % (2 * GW) or tok % 2 or fsdp != 2:
        table = rotary_angles(prefix_len + meta[0] + rows)
        whole = lax.all_gather(prefix_kv, "tok", axis=1, tiled=True)
        pieces, offsets = [], []
        for g in range(width // GW):
            got = attend(scalars(meta, g * GW, g * GW), span, page_len, max_pages, local=(qkv, pool, table), pieces=[whole])
            every = lax.all_gather(got, "fsdp", axis=0)
            for i in range(fsdp):
                pieces.append(every[i])
                offsets.append(i * width + g * GW)
        return project(meta[1], offsets, pieces, dense_weight, dense_bias)

    half = width // 2
    c = lax.axis_index("tok") % 2
    swap_pairs = [(i, i ^ 1) for i in range(tok)]
    ring = chip_ring(tok // 2)
    n = len(ring)
    ahead = [(2 * ring[i] + k, 2 * ring[(i + 1) % n] + k) for i in range(n) for k in range(2)]
    back = [(b, a) for a, b in ahead]

    def swap(x):
        return lax.ppermute(x, "tok", swap_pairs)

    def part(x, which):
        return lax.dynamic_slice_in_dim(x, which * half, half, x.ndim - 1)

    meta2 = swap(meta)
    mine = jnp.concatenate([part(prefix_kv, c), swap(part(prefix_kv, 1 - c))], axis=1)
    hop = {1: (lax.ppermute(mine, "tok", ahead), lax.ppermute(mine, "tok", back))}
    mates = {0: (meta, qkv, pool, rotary_angles(prefix_len + meta[0] + rows))}
    groups = [g * GW for g in range(half // GW)]
    units = [(who, col) for who in (0, 1) for col in groups]
    steps = n // 2
    carries = {}
    for i, (who, col) in enumerate(units):
        m, a, b, t = mates[who]
        s = scalars(m, col if who else c * half + col, col, (1 - c) * half)
        s = s if i else order(s, mine[:, -1:])
        got = attend(s, span, page_len, max_pages, local=(a, b, t), send=0 if i else half)
        if not i:
            mates[1] = (meta2, swap(got[2]), swap(got[3]), rotary_angles(prefix_len + meta2[0] + rows))
        carries[who, col] = got[:2]
        d = i + 2
        if d <= steps:
            fw, bw = hop[d - 1]
            fw, bw, carries[who, col] = lax.optimization_barrier((fw, bw, carries[who, col]))
            hop[d] = (lax.ppermute(fw, "tok", ahead),)
            if d < steps:
                hop[d] += (lax.ppermute(bw, "tok", back),)
    pieces = [mine] + [x for d in range(1, steps + 1) for x in hop[d]]
    ypairs = [(0, 1), (1, 0)]
    proj, offsets, early = [], [], []
    for who, col in [(w, col) for w in (1, 0) for col in groups]:
        s = scalars(mates[who][0], 0, col)
        s = s if who else order(s, *early)
        got = attend(s, span, page_len, max_pages, carry=carries[who, col], pieces=pieces)
        if who:
            early.append(got)
        far = lax.ppermute(got, "fsdp", ypairs)
        if who:
            got, far = swap(got), swap(far)
        at = (1 - c if who else c) * half + col
        proj += [got, far]
        offsets += [f * width + at, (1 - f) * width + at]
    return project(meta[1], offsets, proj, dense_weight, dense_bias)


def solution(mesh):
    return jax.shard_map(
        local_fn,
        mesh=mesh,
        in_specs=(
            P("tok", None, "fsdp"),
            P(None, "tok", "fsdp"),
            P("tok", None, None, None, "fsdp"),
            P("tok", None),
            P("tok"),
            P("tok"),
            P(None, "fsdp"),
            P("fsdp"),
        ),
        out_specs=P("tok", "fsdp"),
        check_vma=False,
    )
```

```python
import functools
import math

import jax
import jax.numpy as jnp
from jax import lax
from jax.experimental import pallas as pl
from jax.experimental.pallas import tpu as pltpu
from jax.sharding import PartitionSpec as P

HD = 96
ROT = 24
LANES = 128
GROUP = 4
GW = GROUP * HD
NEG = -1e30
f32, bf16 = jnp.float32, jnp.bfloat16
SCALE = HD ** -0.5 * math.log2(math.e)
SUM, TOP = HD, HD + 1
STEP = 128
HEAD = 5


def realign(x, h):
    lo = h * HD
    first = lo // LANES * LANES
    off = lo - first
    if off == 0:
        return x[:, first:first + LANES]
    if off + HD <= LANES:
        return pltpu.roll(x[:, first:first + LANES], LANES - off, 1)
    return pltpu.roll(x[:, first:first + 2 * LANES], 2 * LANES - off, 1)[:, :LANES]


def attend_kernel(scal, *rest, local, prefix, send, piece, span, page_len, max_pages, bq, bk):
    it = iter(rest)
    if local:
        qkv, pool, angles = next(it), next(it), next(it)
    else:
        qh, st = next(it), next(it)
    pieces = [next(it) for _ in piece] if prefix else []
    if prefix:
        out = next(it)
    if local:
        qh = next(it)
        if not prefix:
            st = next(it)
        if send:
            qkv_out, pool_out = next(it), next(it)
        qk, sem_q, sem_c = next(it), next(it), next(it)
        if send:
            qkv_held, pool_held, sem_s, sem_t = next(it), next(it), next(it), next(it)
    kb, vb, kh, vh = next(it), next(it), next(it), next(it)
    if prefix:
        sem_p = next(it)
    cached = scal[0]
    live = scal[1]
    cols = pl.ds(pl.multiple_of(scal[2], LANES), GW)
    pcol = pl.ds(pl.multiple_of(scal[3], LANES), GW)
    n_pages = pl.cdiv(cached, page_len)
    base_c = span if local else 0
    base_p = span + max_pages * page_len if local else 0
    per = bk // page_len
    n_cb = pl.cdiv(cached, bk)
    n_full = cached // bk
    heads = range(GROUP)
    zero = jnp.zeros((STEP, LANES), bf16)

    def put_v(at, v):
        lane = lax.broadcasted_iota(jnp.int32, (STEP, LANES), 1)
        one = jnp.where(lane == SUM, 1.0, 0.0).astype(bf16)
        for h in heads:
            vh[h, pl.ds(at, STEP), :] = jnp.where(lane < HD, realign(v, h), one)

    def put_k(at, k):
        for h in heads:
            kh[h, pl.ds(at, STEP), :] = realign(k, h)

    if local:
        new_copies = [
            pltpu.make_async_copy(qkv.at[0, :, cols], qk.at[0], sem_q.at[0]),
            pltpu.make_async_copy(qkv.at[1, :, cols], qk.at[1], sem_q.at[1]),
            pltpu.make_async_copy(qkv.at[2, :, cols], vb.at[pl.ds(0, span), :], sem_q.at[2]),
        ]
        for c in new_copies:
            c.start()

        def page_copies(g):
            dst = pl.ds(pl.multiple_of(base_c + g * page_len, page_len), page_len)
            return (pltpu.make_async_copy(pool.at[scal[HEAD + g], 0, :, cols], kb.at[dst, :], sem_c.at[0, g]),
                    pltpu.make_async_copy(pool.at[scal[HEAD + g], 1, :, cols], vb.at[dst, :], sem_c.at[1, g]))

        def start_page(g, c):
            for x in page_copies(g):
                x.start()
            return c
        lax.fori_loop(0, n_pages, start_page, 0)

        if send:
            scol = pl.ds(pl.multiple_of(scal[4], LANES), qkv_out.shape[2])
            qkv_take = pltpu.make_async_copy(qkv.at[:, :, scol], qkv_held, sem_s)
            qkv_give = pltpu.make_async_copy(qkv_held, qkv_out, sem_s)

            def page_take(g):
                page = scal[HEAD + g]
                return pltpu.make_async_copy(pool.at[page, :, :, scol], pool_held.at[g], sem_t.at[g])

            def page_give(g):
                page = scal[HEAD + g]
                return pltpu.make_async_copy(pool_held.at[g], pool_out.at[page], sem_t.at[g])

            def take(g, c):
                page_take(g).start()
                return c

            def give(g, c):
                page_take(g).wait()
                page_give(g).start()
                return c

            def gone(g, c):
                page_give(g).wait()
                return c
            qkv_take.start()
            lax.fori_loop(0, n_pages, take, 0)

    def piece_copies(i):
        at, n = piece[i]
        dst = pl.ds(base_p + at, n)
        return (pltpu.make_async_copy(pieces[i].at[0, :, pcol], kb.at[dst, :], sem_p.at[0, i]),
                pltpu.make_async_copy(pieces[i].at[1, :, pcol], vb.at[dst, :], sem_p.at[1, i]))

    if prefix:
        for i in range(len(piece)):
            for x in piece_copies(i):
                x.start()

    if local:
        for c in new_copies:
            c.wait()

        def prep_new(j, c):
            at = pl.multiple_of(j * STEP, STEP)
            r = pl.ds(at, STEP)
            lane = lax.broadcasted_iota(jnp.int32, (STEP, LANES), 1)
            cosine, sine = angles[0, r, :], angles[1, r, :]

            def turn(x, h):
                x = realign(x, h).astype(f32)
                mate = jnp.where(lane < ROT // 2, pltpu.roll(x, LANES - ROT // 2, 1), pltpu.roll(x, ROT // 2, 1))
                x = x * cosine + mate * sine
                return jnp.where(lane < HD, x, 0.0).astype(bf16)
            q, k = qk[0, r, :], qk[1, r, :]
            for h in heads:
                qh[h, r, :] = turn(q, h)
                kh[h, r, :] = turn(k, h)
            put_v(at, vb[r, :])
            return c
        n_new = pl.cdiv(live, STEP)
        lax.fori_loop(0, n_new, prep_new, 0)

        def clear_new(j, c):
            r = pl.ds(pl.multiple_of(j * STEP, STEP), STEP)
            for h in heads:
                vh[h, r, :] = zero
            return c
        lax.fori_loop(n_new, span // STEP, clear_new, 0)

        def prep_page(g, c):
            at = pl.multiple_of(base_c + g * page_len, page_len)

            @pl.when(g < n_pages)
            def _():
                for x in page_copies(g):
                    x.wait()
                put_k(at, kb[pl.ds(at, page_len), :])
                put_v(at, vb[pl.ds(at, page_len), :])

            @pl.when(g >= n_pages)
            def _():
                for h in heads:
                    kh[h, pl.ds(at, page_len), :] = zero
                    vh[h, pl.ds(at, page_len), :] = zero
            return c
        lax.fori_loop(0, n_cb * per, prep_page, 0)
        if send:
            qkv_take.wait()
            qkv_give.start()
            lax.fori_loop(0, n_pages, give, 0)

    if prefix:
        for i in range(len(piece)):
            for x in piece_copies(i):
                x.wait()
        total_p = sum(n for _, n in piece)

        def prep_prefix(j, c):
            at = pl.multiple_of(base_p + j * STEP, STEP)
            put_k(at, kb[pl.ds(at, STEP), :])
            put_v(at, vb[pl.ds(at, STEP), :])
            return c
        lax.fori_loop(0, total_p // STEP, prep_prefix, 0)

    def dots(q, h, start, n):
        return lax.dot_general(q, kh[h, pl.ds(start, n), :], (((1,), (1,)), ((), ())), preferred_element_type=f32)

    def fold(state, s, h, start, n):
        top = jnp.max(s, axis=1, keepdims=True)
        new = top if state is None else jnp.maximum(state[0], top)
        p = jnp.exp2((s - new) * SCALE).astype(bf16)
        add = jnp.dot(p, vh[h, pl.ds(start, n), :], preferred_element_type=f32)
        return new, add if state is None else state[1] * jnp.exp2((state[0] - new) * SCALE) + add

    def tile(qt, carry):
        at = pl.multiple_of(qt * bq, bq)
        rows = pl.ds(at, bq)
        qs = [qh[h, rows, :] for h in heads]
        if local:
            seen = lax.broadcasted_iota(jnp.int32, (bq, span), 1) <= lax.broadcasted_iota(jnp.int32, (bq, span), 0) + at
            ss = [dots(q, h, 0, span) for q, h in zip(qs, heads)]
            states = [fold(None, jnp.where(seen, s, NEG), h, 0, span) for s, h in zip(ss, heads)]

            def cache_block(masked, j, sts):
                start = pl.multiple_of(base_c + j * bk, math.gcd(base_c, bk))
                ss = [dots(q, h, start, bk) for q, h in zip(qs, heads)]
                if masked:
                    ok = lax.broadcasted_iota(jnp.int32, (bq, bk), 1) < cached - j * bk
                    ss = [jnp.where(ok, s, NEG) for s in ss]
                return tuple(fold(sx, s, h, start, bk) for sx, s, h in zip(sts, ss, heads))
            states = lax.fori_loop(0, n_full, functools.partial(cache_block, False), tuple(states))
            states = lax.fori_loop(n_full, n_cb, functools.partial(cache_block, True), states)
        else:
            accs = [st[h, rows, :] for h in heads]
            states = [(a[:, TOP:TOP + 1], a) for a in accs]
        if prefix:
            nb = total_p // bk
            for j in range(nb):
                ss = [dots(q, h, base_p + j * bk, bk) for q, h in zip(qs, heads)]
                states = [fold(sx, s, h, base_p + j * bk, bk) for sx, s, h in zip(states, ss, heads)]
            out[rows, :] = jnp.concatenate([(acc / acc[:, SUM:SUM + 1])[:, :HD] for _, acc in states],
                                           axis=1).astype(bf16)
        else:
            lane = lax.broadcasted_iota(jnp.int32, (bq, LANES), 1)
            for h, (m, acc) in zip(heads, states):
                st[h, rows, :] = jnp.where(lane == TOP, m, acc)
        return carry

    lax.fori_loop(0, pl.cdiv(live, bq), tile, 0)

    if send:
        qkv_give.wait()
        lax.fori_loop(0, n_pages, gone, 0)


def attend(scal, span, page_len, max_pages, local=None, carry=None, pieces=None, send=0, bq=256):
    info, at = [], 0
    for p in pieces or []:
        info.append((at, p.shape[1]))
        at += p.shape[1]
    bq = math.gcd(span, bq)
    bk = math.gcd(1024, max_pages * page_len) if local else math.gcd(2048, at)
    if local and pieces:
        bk = math.gcd(bk, at)
    keys = (span + max_pages * page_len if local else 0) + at
    any_ = pl.BlockSpec(memory_space=pltpu.HBM)
    smem = pl.BlockSpec(memory_space=pltpu.SMEM)
    vmem = pl.BlockSpec(memory_space=pltpu.VMEM)
    heads = jax.ShapeDtypeStruct((GROUP, span, LANES), bf16)
    state = jax.ShapeDtypeStruct((GROUP, span, LANES), f32)
    args, in_specs, outs, scratch = [scal], [smem], [], []
    if local:
        args += list(local)
        in_specs += [any_, any_, vmem]
    else:
        args += list(carry)
        in_specs += [vmem] * 2
    if pieces:
        args += list(pieces)
        in_specs += [any_] * len(pieces)
        outs.append(jax.ShapeDtypeStruct((span, GW), bf16))
    if local:
        if pieces:
            scratch.append(pltpu.VMEM(heads.shape, bf16))
        else:
            outs += [heads, state]
            if send:
                outs += [jax.ShapeDtypeStruct((3, span, send), bf16),
                         jax.ShapeDtypeStruct((max_pages, 2, page_len, send), bf16)]
        scratch += [
            pltpu.VMEM((2, span, GW), bf16),
            pltpu.SemaphoreType.DMA((3,)),
            pltpu.SemaphoreType.DMA((2, max_pages)),
        ]
        if send:
            scratch += [pltpu.VMEM((3, span, send), bf16), pltpu.VMEM((max_pages, 2, page_len, send), bf16),
                        pltpu.SemaphoreType.DMA, pltpu.SemaphoreType.DMA((max_pages,))]
    scratch += [pltpu.VMEM((keys, GW), bf16)] * 2 + [pltpu.VMEM((GROUP, keys, LANES), bf16)] * 2
    if pieces:
        scratch += [pltpu.SemaphoreType.DMA((2, len(pieces)))]
    res = pl.pallas_call(
        functools.partial(attend_kernel, local=bool(local), prefix=bool(pieces), send=bool(send), piece=info, span=span, page_len=page_len,
                          max_pages=max_pages, bq=bq, bk=bk),
        out_shape=outs,
        in_specs=in_specs,
        out_specs=[vmem] * (len(outs) - 2 * bool(send)) + [any_] * (2 * bool(send)),
        scratch_shapes=scratch,
        compiler_params=pltpu.CompilerParams(vmem_limit_bytes=56 << 20),
        cost_estimate=pl.CostEstimate(flops=8 * span * keys * GROUP * 2 * LANES, bytes_accessed=8 << 20,
                                      transcendentals=span * keys * GROUP),
        name="attend_" + "new" * bool(local) + "prefix" * bool(pieces),
    )(*args)
    return res[0] if pieces else tuple(res)


def project_kernel(scal, *rest, n, bq, depth):
    pieces, w, bias, out, held = rest[:n], rest[n], rest[n + 1], rest[n + 2], rest[n + 3]
    live = scal[0]
    span, cols = out.shape

    @pl.when(pl.program_id(0) == 0)
    def _():
        for i in range(n):
            held[:, pl.ds(pl.multiple_of(scal[1 + i], LANES), depth)] = pieces[i][...]

    for k in range(1, span // bq + 1):
        @pl.when(pl.cdiv(live, bq) == k)
        def _():
            acc = jnp.dot(held[0:k * bq, :], w[...], preferred_element_type=f32) + bias[...]
            ok = lax.broadcasted_iota(jnp.int32, acc.shape, 0) < live
            out[0:k * bq, :] = jnp.where(ok, acc, 0.0).astype(bf16)
            if k * bq < span:
                out[k * bq:span, :] = jnp.zeros((span - k * bq, cols), bf16)


def project(live, offsets, pieces, weight, bias):
    span, depth = pieces[0].shape
    k, cols = weight.shape
    bn = math.gcd(cols, 512)
    n = len(pieces)
    scal = jnp.stack([jnp.asarray(x, jnp.int32) for x in [live] + list(offsets)])
    return pl.pallas_call(
        functools.partial(project_kernel, n=n, bq=math.gcd(span, 256), depth=depth),
        grid=(cols // bn,),
        out_shape=jax.ShapeDtypeStruct((span, cols), bf16),
        in_specs=[pl.BlockSpec(memory_space=pltpu.SMEM)]
        + [pl.BlockSpec((span, depth), lambda j: (0, 0), pipeline_mode=pl.Buffered(1))] * n
        + [pl.BlockSpec((k, bn), lambda j: (0, j)), pl.BlockSpec((1, bn), lambda j: (0, j))],
        out_specs=pl.BlockSpec((span, bn), lambda j: (0, j)),
        scratch_shapes=[pltpu.VMEM((span, k), bf16)],
        compiler_params=pltpu.CompilerParams(vmem_limit_bytes=48 << 20),
        cost_estimate=pl.CostEstimate(flops=2 * span * k * cols, bytes_accessed=2 * (k * cols + span * (k + cols)),
                                      transcendentals=0),
        name="project",
    )(scal, *pieces, weight, bias.reshape(1, cols))


def rotary_angles(positions):
    half = ROT // 2
    inv = jnp.power(10000.0, -jnp.arange(half, dtype=f32) * 2.0 / ROT)
    inv = jnp.concatenate([inv, inv, jnp.zeros(LANES - ROT, f32)])
    ang = positions.astype(f32)[:, None] * inv[None, :]
    sign = jnp.where(jnp.arange(LANES) < half, -1.0, 1.0)
    return jnp.stack([jnp.cos(ang), jnp.sin(ang) * sign])


def chip_ring(chips):
    if chips == 8:
        return [2 * z for z in range(4)] + [2 * z + 1 for z in (3, 2, 1, 0)]
    return list(range(chips))


def order(scal, *firsts):
    for x in firsts:
        scal = scal + (x[(slice(0, 1),) * x.ndim].reshape(()).astype(f32) > 1e30).astype(jnp.int32)
    return scal


def local_fn(qkv, prefix_kv, cache_pool, page_table, cached_lens, span_lens, dense_weight, dense_bias):
    tok, fsdp = lax.axis_size("tok"), lax.axis_size("fsdp")
    span, _, width = qkv.shape
    qkv = jnp.transpose(qkv, (1, 0, 2))
    pool = cache_pool[0]
    max_pages, _, page_len, _ = pool.shape
    prefix_len = prefix_kv.shape[1] * tok
    f = lax.axis_index("fsdp")
    meta = jnp.concatenate([cached_lens, span_lens, page_table[0]])
    rows = jnp.arange(span, dtype=jnp.int32)

    def scalars(m, col, pcol, scol=0):
        return jnp.concatenate([m[:2], jnp.stack([jnp.asarray(x, jnp.int32) for x in (col, pcol, scol)]), m[2:]])

    if width % (2 * GW) or tok % 2 or fsdp != 2:
        table = rotary_angles(prefix_len + meta[0] + rows)
        whole = lax.all_gather(prefix_kv, "tok", axis=1, tiled=True)
        pieces, offsets = [], []
        for g in range(width // GW):
            got = attend(scalars(meta, g * GW, g * GW), span, page_len, max_pages, local=(qkv, pool, table), pieces=[whole])
            every = lax.all_gather(got, "fsdp", axis=0)
            for i in range(fsdp):
                pieces.append(every[i])
                offsets.append(i * width + g * GW)
        return project(meta[1], offsets, pieces, dense_weight, dense_bias)

    half = width // 2
    c = lax.axis_index("tok") % 2
    swap_pairs = [(i, i ^ 1) for i in range(tok)]
    ring = chip_ring(tok // 2)
    n = len(ring)
    ahead = [(2 * ring[i] + k, 2 * ring[(i + 1) % n] + k) for i in range(n) for k in range(2)]
    back = [(b, a) for a, b in ahead]

    def swap(x):
        return lax.ppermute(x, "tok", swap_pairs)

    def part(x, which):
        return lax.dynamic_slice_in_dim(x, which * half, half, x.ndim - 1)

    meta2 = swap(meta)
    mine = jnp.concatenate([part(prefix_kv, c), swap(part(prefix_kv, 1 - c))], axis=1)
    hop = {1: (lax.ppermute(mine, "tok", ahead), lax.ppermute(mine, "tok", back))}
    mates = {0: (meta, qkv, pool, rotary_angles(prefix_len + meta[0] + rows))}
    groups = [g * GW for g in range(half // GW)]
    units = [(who, col) for who in (0, 1) for col in groups]
    steps = n // 2
    carries = {}
    for i, (who, col) in enumerate(units):
        m, a, b, t = mates[who]
        s = scalars(m, col if who else c * half + col, col, (1 - c) * half)
        s = s if i else order(s, mine[:, -1:])
        got = attend(s, span, page_len, max_pages, local=(a, b, t), send=0 if i else half)
        if not i:
            mates[1] = (meta2, swap(got[2]), swap(got[3]), rotary_angles(prefix_len + meta2[0] + rows))
        carries[who, col] = got[:2]
        d = i + 2
        if d <= steps:
            fw, bw = hop[d - 1]
            fw, bw, carries[who, col] = lax.optimization_barrier((fw, bw, carries[who, col]))
            hop[d] = (lax.ppermute(fw, "tok", ahead),)
            if d < steps:
                hop[d] += (lax.ppermute(bw, "tok", back),)
    pieces = [mine] + [x for d in range(1, steps + 1) for x in hop[d]]
    ypairs = [(0, 1), (1, 0)]
    proj, offsets, early = [], [], []
    for who, col in [(w, col) for w in (1, 0) for col in groups]:
        s = scalars(mates[who][0], 0, col)
        s = s if who else order(s, *early)
        got = attend(s, span, page_len, max_pages, carry=carries[who, col], pieces=pieces)
        if who:
            early.append(got)
        far = lax.ppermute(got, "fsdp", ypairs)
        if who:
            got, far = swap(got), swap(far)
        at = (1 - c if who else c) * half + col
        proj += [got, far]
        offsets += [f * width + at, (1 - f) * width + at]
    return project(meta[1], offsets, proj, dense_weight, dense_bias)


def solution(mesh):
    return jax.shard_map(
        local_fn,
        mesh=mesh,
        in_specs=(
            P("tok", None, "fsdp"),
            P(None, "tok", "fsdp"),
            P("tok", None, None, None, "fsdp"),
            P("tok", None),
            P("tok"),
            P("tok"),
            P(None, "fsdp"),
            P("fsdp"),
        ),
        out_specs=P("tok", "fsdp"),
        check_vma=False,
    )
```

```python
import functools
import math

import jax
import jax.numpy as jnp
from jax import lax
from jax.experimental import pallas as pl
from jax.experimental.pallas import tpu as pltpu
from jax.sharding import PartitionSpec as P

HD = 96
ROT = 24
LANES = 128
GROUP = 4
GW = GROUP * HD
NEG = -1e30
f32, bf16 = jnp.float32, jnp.bfloat16
SCALE = HD ** -0.5 * math.log2(math.e)
SUM, TOP = HD, HD + 1
STEP = 128
HEAD = 5


def realign(x, h):
    lo = h * HD
    first = lo // LANES * LANES
    off = lo - first
    if off == 0:
        return x[:, first:first + LANES]
    if off + HD <= LANES:
        return pltpu.roll(x[:, first:first + LANES], LANES - off, 1)
    return pltpu.roll(x[:, first:first + 2 * LANES], 2 * LANES - off, 1)[:, :LANES]


def attend_kernel(scal, *rest, local, prefix, send, piece, span, page_len, max_pages, bq, bk):
    it = iter(rest)
    if local:
        qkv, pool, angles = next(it), next(it), next(it)
    else:
        qh, st = next(it), next(it)
    pieces = [next(it) for _ in piece] if prefix else []
    if prefix:
        out = next(it)
    if local:
        qh = next(it)
        if not prefix:
            st = next(it)
        if send:
            qkv_out, pool_out = next(it), next(it)
        qk, sem_q, sem_c = next(it), next(it), next(it)
        if send:
            qkv_held, pool_held, sem_s, sem_t = next(it), next(it), next(it), next(it)
    kb, vb, kh, vh = next(it), next(it), next(it), next(it)
    if prefix:
        sem_p = next(it)
    cached = scal[0]
    live = scal[1]
    cols = pl.ds(pl.multiple_of(scal[2], LANES), GW)
    pcol = pl.ds(pl.multiple_of(scal[3], LANES), GW)
    n_pages = pl.cdiv(cached, page_len)
    base_c = span if local else 0
    base_p = span + max_pages * page_len if local else 0
    per = bk // page_len
    n_cb = pl.cdiv(cached, bk)
    n_full = cached // bk
    heads = range(GROUP)
    zero = jnp.zeros((STEP, LANES), bf16)

    def put_v(at, v):
        lane = lax.broadcasted_iota(jnp.int32, (STEP, LANES), 1)
        one = jnp.where(lane == SUM, 1.0, 0.0).astype(bf16)
        for h in heads:
            vh[h, pl.ds(at, STEP), :] = jnp.where(lane < HD, realign(v, h), one)

    def put_k(at, k):
        for h in heads:
            kh[h, pl.ds(at, STEP), :] = realign(k, h)

    if local:
        new_copies = [
            pltpu.make_async_copy(qkv.at[0, :, cols], qk.at[0], sem_q.at[0]),
            pltpu.make_async_copy(qkv.at[1, :, cols], qk.at[1], sem_q.at[1]),
            pltpu.make_async_copy(qkv.at[2, :, cols], vb.at[pl.ds(0, span), :], sem_q.at[2]),
        ]
        for c in new_copies:
            c.start()

        def page_copies(g):
            dst = pl.ds(pl.multiple_of(base_c + g * page_len, page_len), page_len)
            return (pltpu.make_async_copy(pool.at[scal[HEAD + g], 0, :, cols], kb.at[dst, :], sem_c.at[0, g]),
                    pltpu.make_async_copy(pool.at[scal[HEAD + g], 1, :, cols], vb.at[dst, :], sem_c.at[1, g]))

        def start_page(g, c):
            for x in page_copies(g):
                x.start()
            return c
        lax.fori_loop(0, n_pages, start_page, 0)

        if send:
            scol = pl.ds(pl.multiple_of(scal[4], LANES), qkv_out.shape[2])
            qkv_take = pltpu.make_async_copy(qkv.at[:, :, scol], qkv_held, sem_s)
            qkv_give = pltpu.make_async_copy(qkv_held, qkv_out, sem_s)

            def page_take(g):
                page = scal[HEAD + g]
                return pltpu.make_async_copy(pool.at[page, :, :, scol], pool_held.at[g], sem_t.at[g])

            def page_give(g):
                page = scal[HEAD + g]
                return pltpu.make_async_copy(pool_held.at[g], pool_out.at[page], sem_t.at[g])

            def take(g, c):
                page_take(g).start()
                return c

            def give(g, c):
                page_take(g).wait()
                page_give(g).start()
                return c

            def gone(g, c):
                page_give(g).wait()
                return c
            qkv_take.start()
            lax.fori_loop(0, n_pages, take, 0)

    def piece_copies(i):
        at, n = piece[i]
        dst = pl.ds(base_p + at, n)
        return (pltpu.make_async_copy(pieces[i].at[0, :, pcol], kb.at[dst, :], sem_p.at[0, i]),
                pltpu.make_async_copy(pieces[i].at[1, :, pcol], vb.at[dst, :], sem_p.at[1, i]))

    if prefix:
        for i in range(len(piece)):
            for x in piece_copies(i):
                x.start()

    if local:
        for c in new_copies:
            c.wait()

        def prep_new(j, c):
            at = pl.multiple_of(j * STEP, STEP)
            r = pl.ds(at, STEP)
            lane = lax.broadcasted_iota(jnp.int32, (STEP, LANES), 1)
            cosine, sine = angles[0, r, :], angles[1, r, :]

            def turn(x, h):
                x = realign(x, h).astype(f32)
                mate = jnp.where(lane < ROT // 2, pltpu.roll(x, LANES - ROT // 2, 1), pltpu.roll(x, ROT // 2, 1))
                x = x * cosine + mate * sine
                return jnp.where(lane < HD, x, 0.0).astype(bf16)
            q, k = qk[0, r, :], qk[1, r, :]
            for h in heads:
                qh[h, r, :] = turn(q, h)
                kh[h, r, :] = turn(k, h)
            put_v(at, vb[r, :])
            return c
        n_new = pl.cdiv(live, STEP)
        lax.fori_loop(0, n_new, prep_new, 0)

        def clear_new(j, c):
            r = pl.ds(pl.multiple_of(j * STEP, STEP), STEP)
            for h in heads:
                vh[h, r, :] = zero
            return c
        lax.fori_loop(n_new, span // STEP, clear_new, 0)

        def prep_page(g, c):
            at = pl.multiple_of(base_c + g * page_len, page_len)

            @pl.when(g < n_pages)
            def _():
                for x in page_copies(g):
                    x.wait()
                put_k(at, kb[pl.ds(at, page_len), :])
                put_v(at, vb[pl.ds(at, page_len), :])

            @pl.when(g >= n_pages)
            def _():
                for h in heads:
                    kh[h, pl.ds(at, page_len), :] = zero
                    vh[h, pl.ds(at, page_len), :] = zero
            return c
        lax.fori_loop(0, n_cb * per, prep_page, 0)
        if send:
            qkv_take.wait()
            qkv_give.start()
            lax.fori_loop(0, n_pages, give, 0)

    if prefix:
        for i in range(len(piece)):
            for x in piece_copies(i):
                x.wait()
        total_p = sum(n for _, n in piece)

        def prep_prefix(j, c):
            at = pl.multiple_of(base_p + j * STEP, STEP)
            put_k(at, kb[pl.ds(at, STEP), :])
            put_v(at, vb[pl.ds(at, STEP), :])
            return c
        lax.fori_loop(0, total_p // STEP, prep_prefix, 0)

    def dots(q, h, start, n):
        return lax.dot_general(q, kh[h, pl.ds(start, n), :], (((1,), (1,)), ((), ())), preferred_element_type=f32)

    def fold(state, s, h, start, n):
        top = jnp.max(s, axis=1, keepdims=True)
        new = top if state is None else jnp.maximum(state[0], top)
        p = jnp.exp2((s - new) * SCALE).astype(bf16)
        add = jnp.dot(p, vh[h, pl.ds(start, n), :], preferred_element_type=f32)
        return new, add if state is None else state[1] * jnp.exp2((state[0] - new) * SCALE) + add

    def tile(qt, carry):
        at = pl.multiple_of(qt * bq, bq)
        rows = pl.ds(at, bq)
        qs = [qh[h, rows, :] for h in heads]
        if local:
            seen = lax.broadcasted_iota(jnp.int32, (bq, span), 1) <= lax.broadcasted_iota(jnp.int32, (bq, span), 0) + at
            ss = [dots(q, h, 0, span) for q, h in zip(qs, heads)]
            states = [fold(None, jnp.where(seen, s, NEG), h, 0, span) for s, h in zip(ss, heads)]

            def cache_block(masked, j, sts):
                start = pl.multiple_of(base_c + j * bk, math.gcd(base_c, bk))
                ss = [dots(q, h, start, bk) for q, h in zip(qs, heads)]
                if masked:
                    ok = lax.broadcasted_iota(jnp.int32, (bq, bk), 1) < cached - j * bk
                    ss = [jnp.where(ok, s, NEG) for s in ss]
                return tuple(fold(sx, s, h, start, bk) for sx, s, h in zip(sts, ss, heads))
            states = lax.fori_loop(0, n_full, functools.partial(cache_block, False), tuple(states))
            states = lax.fori_loop(n_full, n_cb, functools.partial(cache_block, True), states)
        else:
            accs = [st[h, rows, :] for h in heads]
            states = [(a[:, TOP:TOP + 1], a) for a in accs]
        if prefix:
            nb = total_p // bk
            for j in range(nb):
                ss = [dots(q, h, base_p + j * bk, bk) for q, h in zip(qs, heads)]
                states = [fold(sx, s, h, base_p + j * bk, bk) for sx, s, h in zip(states, ss, heads)]
            out[rows, :] = jnp.concatenate([(acc / acc[:, SUM:SUM + 1])[:, :HD] for _, acc in states],
                                           axis=1).astype(bf16)
        else:
            lane = lax.broadcasted_iota(jnp.int32, (bq, LANES), 1)
            for h, (m, acc) in zip(heads, states):
                st[h, rows, :] = jnp.where(lane == TOP, m, acc)
        return carry

    lax.fori_loop(0, pl.cdiv(live, bq), tile, 0)

    if send:
        qkv_give.wait()
        lax.fori_loop(0, n_pages, gone, 0)


def attend(scal, span, page_len, max_pages, local=None, carry=None, pieces=None, send=0, bq=256):
    info, at = [], 0
    for p in pieces or []:
        info.append((at, p.shape[1]))
        at += p.shape[1]
    bq = math.gcd(span, bq)
    bk = math.gcd(1024, max_pages * page_len) if local else math.gcd(2048, at)
    if local and pieces:
        bk = math.gcd(bk, at)
    keys = (span + max_pages * page_len if local else 0) + at
    any_ = pl.BlockSpec(memory_space=pltpu.HBM)
    smem = pl.BlockSpec(memory_space=pltpu.SMEM)
    vmem = pl.BlockSpec(memory_space=pltpu.VMEM)
    heads = jax.ShapeDtypeStruct((GROUP, span, LANES), bf16)
    state = jax.ShapeDtypeStruct((GROUP, span, LANES), f32)
    args, in_specs, outs, scratch = [scal], [smem], [], []
    if local:
        args += list(local)
        in_specs += [any_, any_, vmem]
    else:
        args += list(carry)
        in_specs += [vmem] * 2
    if pieces:
        args += list(pieces)
        in_specs += [any_] * len(pieces)
        outs.append(jax.ShapeDtypeStruct((span, GW), bf16))
    if local:
        if pieces:
            scratch.append(pltpu.VMEM(heads.shape, bf16))
        else:
            outs += [heads, state]
            if send:
                outs += [jax.ShapeDtypeStruct((3, span, send), bf16),
                         jax.ShapeDtypeStruct((max_pages, 2, page_len, send), bf16)]
        scratch += [
            pltpu.VMEM((2, span, GW), bf16),
            pltpu.SemaphoreType.DMA((3,)),
            pltpu.SemaphoreType.DMA((2, max_pages)),
        ]
        if send:
            scratch += [pltpu.VMEM((3, span, send), bf16), pltpu.VMEM((max_pages, 2, page_len, send), bf16),
                        pltpu.SemaphoreType.DMA, pltpu.SemaphoreType.DMA((max_pages,))]
    scratch += [pltpu.VMEM((keys, GW), bf16)] * 2 + [pltpu.VMEM((GROUP, keys, LANES), bf16)] * 2
    if pieces:
        scratch += [pltpu.SemaphoreType.DMA((2, len(pieces)))]
    res = pl.pallas_call(
        functools.partial(attend_kernel, local=bool(local), prefix=bool(pieces), send=bool(send), piece=info, span=span, page_len=page_len,
                          max_pages=max_pages, bq=bq, bk=bk),
        out_shape=outs,
        in_specs=in_specs,
        out_specs=[vmem] * (len(outs) - 2 * bool(send)) + [any_] * (2 * bool(send)),
        scratch_shapes=scratch,
        compiler_params=pltpu.CompilerParams(vmem_limit_bytes=56 << 20),
        cost_estimate=pl.CostEstimate(flops=40 * span * keys * GROUP * 2 * LANES, bytes_accessed=8 << 20,
                                      transcendentals=span * keys * GROUP),
        name="attend_" + "new" * bool(local) + "prefix" * bool(pieces),
    )(*args)
    return res[0] if pieces else tuple(res)


def project_kernel(scal, *rest, n, bq, depth):
    pieces, w, bias, out, held = rest[:n], rest[n], rest[n + 1], rest[n + 2], rest[n + 3]
    live = scal[0]
    span, cols = out.shape

    @pl.when(pl.program_id(0) == 0)
    def _():
        for i in range(n):
            held[:, pl.ds(pl.multiple_of(scal[1 + i], LANES), depth)] = pieces[i][...]

    for k in range(1, span // bq + 1):
        @pl.when(pl.cdiv(live, bq) == k)
        def _():
            acc = jnp.dot(held[0:k * bq, :], w[...], preferred_element_type=f32) + bias[...]
            ok = lax.broadcasted_iota(jnp.int32, acc.shape, 0) < live
            out[0:k * bq, :] = jnp.where(ok, acc, 0.0).astype(bf16)
            if k * bq < span:
                out[k * bq:span, :] = jnp.zeros((span - k * bq, cols), bf16)


def project(live, offsets, pieces, weight, bias):
    span, depth = pieces[0].shape
    k, cols = weight.shape
    bn = math.gcd(cols, 512)
    n = len(pieces)
    scal = jnp.stack([jnp.asarray(x, jnp.int32) for x in [live] + list(offsets)])
    return pl.pallas_call(
        functools.partial(project_kernel, n=n, bq=math.gcd(span, 256), depth=depth),
        grid=(cols // bn,),
        out_shape=jax.ShapeDtypeStruct((span, cols), bf16),
        in_specs=[pl.BlockSpec(memory_space=pltpu.SMEM)]
        + [pl.BlockSpec((span, depth), lambda j: (0, 0), pipeline_mode=pl.Buffered(1))] * n
        + [pl.BlockSpec((k, bn), lambda j: (0, j)), pl.BlockSpec((1, bn), lambda j: (0, j))],
        out_specs=pl.BlockSpec((span, bn), lambda j: (0, j)),
        scratch_shapes=[pltpu.VMEM((span, k), bf16)],
        compiler_params=pltpu.CompilerParams(vmem_limit_bytes=48 << 20),
        cost_estimate=pl.CostEstimate(flops=2 * span * k * cols, bytes_accessed=2 * (k * cols + span * (k + cols)),
                                      transcendentals=0),
        name="project",
    )(scal, *pieces, weight, bias.reshape(1, cols))


def rotary_angles(positions):
    half = ROT // 2
    inv = jnp.power(10000.0, -jnp.arange(half, dtype=f32) * 2.0 / ROT)
    inv = jnp.concatenate([inv, inv, jnp.zeros(LANES - ROT, f32)])
    ang = positions.astype(f32)[:, None] * inv[None, :]
    sign = jnp.where(jnp.arange(LANES) < half, -1.0, 1.0)
    return jnp.stack([jnp.cos(ang), jnp.sin(ang) * sign])


def chip_ring(chips):
    if chips == 8:
        return [2 * z for z in range(4)] + [2 * z + 1 for z in (3, 2, 1, 0)]
    return list(range(chips))


def order(scal, *firsts):
    for x in firsts:
        scal = scal + (x[(slice(0, 1),) * x.ndim].reshape(()).astype(f32) > 1e30).astype(jnp.int32)
    return scal


def local_fn(qkv, prefix_kv, cache_pool, page_table, cached_lens, span_lens, dense_weight, dense_bias):
    tok, fsdp = lax.axis_size("tok"), lax.axis_size("fsdp")
    span, _, width = qkv.shape
    qkv = jnp.transpose(qkv, (1, 0, 2))
    pool = cache_pool[0]
    max_pages, _, page_len, _ = pool.shape
    prefix_len = prefix_kv.shape[1] * tok
    f = lax.axis_index("fsdp")
    meta = jnp.concatenate([cached_lens, span_lens, page_table[0]])
    rows = jnp.arange(span, dtype=jnp.int32)

    def scalars(m, col, pcol, scol=0):
        return jnp.concatenate([m[:2], jnp.stack([jnp.asarray(x, jnp.int32) for x in (col, pcol, scol)]), m[2:]])

    if width % (2 * GW) or tok % 2 or fsdp != 2:
        table = rotary_angles(prefix_len + meta[0] + rows)
        whole = lax.all_gather(prefix_kv, "tok", axis=1, tiled=True)
        pieces, offsets = [], []
        for g in range(width // GW):
            got = attend(scalars(meta, g * GW, g * GW), span, page_len, max_pages, local=(qkv, pool, table), pieces=[whole])
            every = lax.all_gather(got, "fsdp", axis=0)
            for i in range(fsdp):
                pieces.append(every[i])
                offsets.append(i * width + g * GW)
        return project(meta[1], offsets, pieces, dense_weight, dense_bias)

    half = width // 2
    c = lax.axis_index("tok") % 2
    swap_pairs = [(i, i ^ 1) for i in range(tok)]
    ring = chip_ring(tok // 2)
    n = len(ring)
    ahead = [(2 * ring[i] + k, 2 * ring[(i + 1) % n] + k) for i in range(n) for k in range(2)]
    back = [(b, a) for a, b in ahead]

    def swap(x):
        return lax.ppermute(x, "tok", swap_pairs)

    def part(x, which):
        return lax.dynamic_slice_in_dim(x, which * half, half, x.ndim - 1)

    meta2 = swap(meta)
    mine = jnp.concatenate([part(prefix_kv, c), swap(part(prefix_kv, 1 - c))], axis=1)
    hop = {1: (lax.ppermute(mine, "tok", ahead), lax.ppermute(mine, "tok", back))}
    mates = {0: (meta, qkv, pool, rotary_angles(prefix_len + meta[0] + rows))}
    groups = [g * GW for g in range(half // GW)]
    units = [(who, col) for who in (0, 1) for col in groups]
    steps = n // 2
    carries = {}
    for i, (who, col) in enumerate(units):
        m, a, b, t = mates[who]
        s = scalars(m, col if who else c * half + col, col, (1 - c) * half)
        s = s if i else order(s, mine[:, -1:])
        got = attend(s, span, page_len, max_pages, local=(a, b, t), send=0 if i else half)
        if not i:
            mates[1] = (meta2, swap(got[2]), swap(got[3]), rotary_angles(prefix_len + meta2[0] + rows))
        carries[who, col] = got[:2]
        d = i + 2
        if d <= steps:
            fw, bw = hop[d - 1]
            fw, bw, carries[who, col] = lax.optimization_barrier((fw, bw, carries[who, col]))
            hop[d] = (lax.ppermute(fw, "tok", ahead),)
            if d < steps:
                hop[d] += (lax.ppermute(bw, "tok", back),)
    pieces = [mine] + [x for d in range(1, steps + 1) for x in hop[d]]
    ypairs = [(0, 1), (1, 0)]
    proj, offsets, early = [], [], []
    for who, col in [(w, col) for w in (1, 0) for col in groups]:
        s = scalars(mates[who][0], 0, col)
        s = s if who else order(s, *early)
        got = attend(s, span, page_len, max_pages, carry=carries[who, col], pieces=pieces)
        if who:
            early.append(got)
        far = lax.ppermute(got, "fsdp", ypairs)
        if who:
            got, far = swap(got), swap(far)
        at = (1 - c if who else c) * half + col
        proj += [got, far]
        offsets += [f * width + at, (1 - f) * width + at]
    return project(meta[1], offsets, proj, dense_weight, dense_bias)


def solution(mesh):
    return jax.shard_map(
        local_fn,
        mesh=mesh,
        in_specs=(
            P("tok", None, "fsdp"),
            P(None, "tok", "fsdp"),
            P("tok", None, None, None, "fsdp"),
            P("tok", None),
            P("tok"),
            P("tok"),
            P(None, "fsdp"),
            P("fsdp"),
        ),
        out_specs=P("tok", "fsdp"),
        check_vma=False,
    )
```

```python
import functools
import math

import jax
import jax.numpy as jnp
from jax import lax
from jax.experimental import pallas as pl
from jax.experimental.pallas import tpu as pltpu
from jax.sharding import PartitionSpec as P

HD = 96
ROT = 24
LANES = 128
GROUP = 4
GW = GROUP * HD
NEG = -1e30
f32, bf16 = jnp.float32, jnp.bfloat16
SCALE = HD ** -0.5 * math.log2(math.e)
SUM, TOP = HD, HD + 1
STEP = 128
HEAD = 5


def realign(x, h):
    lo = h * HD
    first = lo // LANES * LANES
    off = lo - first
    if off == 0:
        return x[:, first:first + LANES]
    if off + HD <= LANES:
        return pltpu.roll(x[:, first:first + LANES], LANES - off, 1)
    return pltpu.roll(x[:, first:first + 2 * LANES], 2 * LANES - off, 1)[:, :LANES]


def attend_kernel(scal, *rest, local, prefix, send, piece, span, page_len, max_pages, bq, bk):
    it = iter(rest)
    if local:
        qkv, pool, angles = next(it), next(it), next(it)
    else:
        qh, st = next(it), next(it)
    pieces = [next(it) for _ in piece] if prefix else []
    if prefix:
        out = next(it)
    if local:
        qh = next(it)
        if not prefix:
            st = next(it)
        if send:
            qkv_out, pool_out = next(it), next(it)
        qk, sem_q, sem_c = next(it), next(it), next(it)
        if send:
            qkv_held, pool_held, sem_s, sem_t = next(it), next(it), next(it), next(it)
    kb, vb, kh, vh = next(it), next(it), next(it), next(it)
    if prefix:
        sem_p = next(it)
    cached = scal[0]
    live = scal[1]
    cols = pl.ds(pl.multiple_of(scal[2], LANES), GW)
    pcol = pl.ds(pl.multiple_of(scal[3], LANES), GW)
    n_pages = pl.cdiv(cached, page_len)
    base_c = span if local else 0
    base_p = span + max_pages * page_len if local else 0
    per = bk // page_len
    n_cb = pl.cdiv(cached, bk)
    n_full = cached // bk
    heads = range(GROUP)
    zero = jnp.zeros((STEP, LANES), bf16)

    def put_v(at, v):
        lane = lax.broadcasted_iota(jnp.int32, (STEP, LANES), 1)
        one = jnp.where(lane == SUM, 1.0, 0.0).astype(bf16)
        for h in heads:
            vh[h, pl.ds(at, STEP), :] = jnp.where(lane < HD, realign(v, h), one)

    def put_k(at, k):
        for h in heads:
            kh[h, pl.ds(at, STEP), :] = realign(k, h)

    if local:
        new_copies = [
            pltpu.make_async_copy(qkv.at[0, :, cols], qk.at[0], sem_q.at[0]),
            pltpu.make_async_copy(qkv.at[1, :, cols], qk.at[1], sem_q.at[1]),
            pltpu.make_async_copy(qkv.at[2, :, cols], vb.at[pl.ds(0, span), :], sem_q.at[2]),
        ]
        for c in new_copies:
            c.start()

        def page_copies(g):
            dst = pl.ds(pl.multiple_of(base_c + g * page_len, page_len), page_len)
            return (pltpu.make_async_copy(pool.at[scal[HEAD + g], 0, :, cols], kb.at[dst, :], sem_c.at[0, g]),
                    pltpu.make_async_copy(pool.at[scal[HEAD + g], 1, :, cols], vb.at[dst, :], sem_c.at[1, g]))

        def start_page(g, c):
            for x in page_copies(g):
                x.start()
            return c
        lax.fori_loop(0, n_pages, start_page, 0)

        if send:
            scol = pl.ds(pl.multiple_of(scal[4], LANES), qkv_out.shape[2])
            qkv_take = pltpu.make_async_copy(qkv.at[:, :, scol], qkv_held, sem_s)
            qkv_give = pltpu.make_async_copy(qkv_held, qkv_out, sem_s)

            def page_take(g):
                page = scal[HEAD + g]
                return pltpu.make_async_copy(pool.at[page, :, :, scol], pool_held.at[g], sem_t.at[g])

            def page_give(g):
                page = scal[HEAD + g]
                return pltpu.make_async_copy(pool_held.at[g], pool_out.at[page], sem_t.at[g])

            def take(g, c):
                page_take(g).start()
                return c

            def give(g, c):
                page_take(g).wait()
                page_give(g).start()
                return c

            def gone(g, c):
                page_give(g).wait()
                return c
            qkv_take.start()
            lax.fori_loop(0, n_pages, take, 0)

    def piece_copies(i):
        at, n = piece[i]
        dst = pl.ds(base_p + at, n)
        return (pltpu.make_async_copy(pieces[i].at[0, :, pcol], kb.at[dst, :], sem_p.at[0, i]),
                pltpu.make_async_copy(pieces[i].at[1, :, pcol], vb.at[dst, :], sem_p.at[1, i]))

    if prefix:
        for i in range(len(piece)):
            for x in piece_copies(i):
                x.start()

    if local:
        for c in new_copies:
            c.wait()

        def prep_new(j, c):
            at = pl.multiple_of(j * STEP, STEP)
            r = pl.ds(at, STEP)
            lane = lax.broadcasted_iota(jnp.int32, (STEP, LANES), 1)
            cosine, sine = angles[0, r, :], angles[1, r, :]

            def turn(x, h):
                x = realign(x, h).astype(f32)
                mate = jnp.where(lane < ROT // 2, pltpu.roll(x, LANES - ROT // 2, 1), pltpu.roll(x, ROT // 2, 1))
                x = x * cosine + mate * sine
                return jnp.where(lane < HD, x, 0.0).astype(bf16)
            q, k = qk[0, r, :], qk[1, r, :]
            for h in heads:
                qh[h, r, :] = turn(q, h)
                kh[h, r, :] = turn(k, h)
            put_v(at, vb[r, :])
            return c
        n_new = pl.cdiv(live, STEP)
        lax.fori_loop(0, n_new, prep_new, 0)

        def clear_new(j, c):
            r = pl.ds(pl.multiple_of(j * STEP, STEP), STEP)
            for h in heads:
                vh[h, r, :] = zero
            return c
        lax.fori_loop(n_new, span // STEP, clear_new, 0)

        def prep_page(g, c):
            at = pl.multiple_of(base_c + g * page_len, page_len)

            @pl.when(g < n_pages)
            def _():
                for x in page_copies(g):
                    x.wait()
                put_k(at, kb[pl.ds(at, page_len), :])
                put_v(at, vb[pl.ds(at, page_len), :])

            @pl.when(g >= n_pages)
            def _():
                for h in heads:
                    kh[h, pl.ds(at, page_len), :] = zero
                    vh[h, pl.ds(at, page_len), :] = zero
            return c
        lax.fori_loop(0, n_cb * per, prep_page, 0)
        if send:
            qkv_take.wait()
            qkv_give.start()
            lax.fori_loop(0, n_pages, give, 0)

    if prefix:
        for i in range(len(piece)):
            for x in piece_copies(i):
                x.wait()
        total_p = sum(n for _, n in piece)

        def prep_prefix(j, c):
            at = pl.multiple_of(base_p + j * STEP, STEP)
            put_k(at, kb[pl.ds(at, STEP), :])
            put_v(at, vb[pl.ds(at, STEP), :])
            return c
        lax.fori_loop(0, total_p // STEP, prep_prefix, 0)

    def dots(q, h, start, n):
        return lax.dot_general(q, kh[h, pl.ds(start, n), :], (((1,), (1,)), ((), ())), preferred_element_type=f32)

    def fold(state, s, h, start, n):
        top = jnp.max(s, axis=1, keepdims=True)
        new = top if state is None else jnp.maximum(state[0], top)
        p = jnp.exp2((s - new) * SCALE).astype(bf16)
        add = jnp.dot(p, vh[h, pl.ds(start, n), :], preferred_element_type=f32)
        return new, add if state is None else state[1] * jnp.exp2((state[0] - new) * SCALE) + add

    def tile(qt, carry):
        at = pl.multiple_of(qt * bq, bq)
        rows = pl.ds(at, bq)
        qs = [qh[h, rows, :] for h in heads]
        if local:
            seen = lax.broadcasted_iota(jnp.int32, (bq, span), 1) <= lax.broadcasted_iota(jnp.int32, (bq, span), 0) + at
            ss = [dots(q, h, 0, span) for q, h in zip(qs, heads)]
            states = [fold(None, jnp.where(seen, s, NEG), h, 0, span) for s, h in zip(ss, heads)]

            def cache_block(masked, j, sts):
                start = pl.multiple_of(base_c + j * bk, math.gcd(base_c, bk))
                ss = [dots(q, h, start, bk) for q, h in zip(qs, heads)]
                if masked:
                    ok = lax.broadcasted_iota(jnp.int32, (bq, bk), 1) < cached - j * bk
                    ss = [jnp.where(ok, s, NEG) for s in ss]
                return tuple(fold(sx, s, h, start, bk) for sx, s, h in zip(sts, ss, heads))
            states = lax.fori_loop(0, n_full, functools.partial(cache_block, False), tuple(states))
            states = lax.fori_loop(n_full, n_cb, functools.partial(cache_block, True), states)
        else:
            accs = [st[h, rows, :] for h in heads]
            states = [(a[:, TOP:TOP + 1], a) for a in accs]
        if prefix:
            nb = total_p // bk
            for j in range(nb):
                ss = [dots(q, h, base_p + j * bk, bk) for q, h in zip(qs, heads)]
                states = [fold(sx, s, h, base_p + j * bk, bk) for sx, s, h in zip(states, ss, heads)]
            out[rows, :] = jnp.concatenate([(acc / acc[:, SUM:SUM + 1])[:, :HD] for _, acc in states],
                                           axis=1).astype(bf16)
        else:
            lane = lax.broadcasted_iota(jnp.int32, (bq, LANES), 1)
            for h, (m, acc) in zip(heads, states):
                st[h, rows, :] = jnp.where(lane == TOP, m, acc)
        return carry

    lax.fori_loop(0, pl.cdiv(live, bq), tile, 0)

    if send:
        qkv_give.wait()
        lax.fori_loop(0, n_pages, gone, 0)


def attend(scal, span, page_len, max_pages, local=None, carry=None, pieces=None, send=0, bq=256):
    info, at = [], 0
    for p in pieces or []:
        info.append((at, p.shape[1]))
        at += p.shape[1]
    bq = math.gcd(span, bq)
    bk = math.gcd(1024, max_pages * page_len) if local else math.gcd(2048, at)
    if local and pieces:
        bk = math.gcd(bk, at)
    keys = (span + max_pages * page_len if local else 0) + at
    any_ = pl.BlockSpec(memory_space=pltpu.HBM)
    smem = pl.BlockSpec(memory_space=pltpu.SMEM)
    vmem = pl.BlockSpec(memory_space=pltpu.VMEM)
    heads = jax.ShapeDtypeStruct((GROUP, span, LANES), bf16)
    state = jax.ShapeDtypeStruct((GROUP, span, LANES), f32)
    args, in_specs, outs, scratch = [scal], [smem], [], []
    if local:
        args += list(local)
        in_specs += [any_, any_, vmem]
    else:
        args += list(carry)
        in_specs += [vmem] * 2
    if pieces:
        args += list(pieces)
        in_specs += [any_] * len(pieces)
        outs.append(jax.ShapeDtypeStruct((span, GW), bf16))
    if local:
        if pieces:
            scratch.append(pltpu.VMEM(heads.shape, bf16))
        else:
            outs += [heads, state]
            if send:
                outs += [jax.ShapeDtypeStruct((3, span, send), bf16),
                         jax.ShapeDtypeStruct((max_pages, 2, page_len, send), bf16)]
        scratch += [
            pltpu.VMEM((2, span, GW), bf16),
            pltpu.SemaphoreType.DMA((3,)),
            pltpu.SemaphoreType.DMA((2, max_pages)),
        ]
        if send:
            scratch += [pltpu.VMEM((3, span, send), bf16), pltpu.VMEM((max_pages, 2, page_len, send), bf16),
                        pltpu.SemaphoreType.DMA, pltpu.SemaphoreType.DMA((max_pages,))]
    scratch += [pltpu.VMEM((keys, GW), bf16)] * 2 + [pltpu.VMEM((GROUP, keys, LANES), bf16)] * 2
    if pieces:
        scratch += [pltpu.SemaphoreType.DMA((2, len(pieces)))]
    res = pl.pallas_call(
        functools.partial(attend_kernel, local=bool(local), prefix=bool(pieces), send=bool(send), piece=info, span=span, page_len=page_len,
                          max_pages=max_pages, bq=bq, bk=bk),
        out_shape=outs,
        in_specs=in_specs,
        out_specs=[vmem] * (len(outs) - 2 * bool(send)) + [any_] * (2 * bool(send)),
        scratch_shapes=scratch,
        compiler_params=pltpu.CompilerParams(vmem_limit_bytes=56 << 20),
        cost_estimate=pl.CostEstimate(flops=40 * span * keys * GROUP * 2 * LANES, bytes_accessed=8 << 20,
                                      transcendentals=span * keys * GROUP),
        name="attend_" + "new" * bool(local) + "prefix" * bool(pieces),
    )(*args)
    return res[0] if pieces else tuple(res)


def project_kernel(scal, *rest, n, bq, last):
    pieces, w, start, out = rest[:n], rest[n:2 * n], rest[2 * n], rest[2 * n + 1]
    live = scal[0]
    span, cols = out.shape
    for k in range(1, span // bq + 1):
        @pl.when(pl.cdiv(live, bq) == k)
        def _():
            rows = k * bq
            acc = start[0:rows, :] if start.shape[0] > 1 else start[...]
            for x, y in zip(pieces, w):
                acc = acc + jnp.dot(x[0:rows, :], y[...], preferred_element_type=f32)
            if last:
                acc = jnp.where(lax.broadcasted_iota(jnp.int32, acc.shape, 0) < live, acc, 0.0)
            out[0:rows, :] = acc.astype(out.dtype)
            if last and rows < span:
                out[rows:span, :] = jnp.zeros((span - rows, cols), bf16)


def project(live, offsets, pieces, weight, start, last=True):
    span, depth = pieces[0].shape
    cols = weight.shape[1]
    bn = math.gcd(cols, 512)
    n = len(pieces)
    scal = jnp.stack([jnp.asarray(x, jnp.int32) for x in [live] + [o // depth for o in offsets]])
    return pl.pallas_call(
        functools.partial(project_kernel, n=n, bq=math.gcd(span, 256), last=last),
        grid_spec=pltpu.PrefetchScalarGridSpec(
            num_scalar_prefetch=1,
            grid=(cols // bn,),
            in_specs=[pl.BlockSpec((span, depth), lambda j, s: (0, 0), pipeline_mode=pl.Buffered(1))] * n
            + [pl.BlockSpec((depth, bn), lambda j, s, i=i: (s[1 + i], j)) for i in range(n)]
            + [pl.BlockSpec((start.shape[0], bn), lambda j, s: (0, j))],
            out_specs=pl.BlockSpec((span, bn), lambda j, s: (0, j))),
        out_shape=jax.ShapeDtypeStruct((span, cols), bf16 if last else f32),
        compiler_params=pltpu.CompilerParams(vmem_limit_bytes=48 << 20),
        cost_estimate=pl.CostEstimate(flops=2 * span * n * depth * cols, bytes_accessed=2 * cols * (n * depth + 3 * span),
                                      transcendentals=0),
        name="project",
    )(scal, *pieces, *[weight] * n, start)


def rotary_angles(positions):
    half = ROT // 2
    inv = jnp.power(10000.0, -jnp.arange(half, dtype=f32) * 2.0 / ROT)
    inv = jnp.concatenate([inv, inv, jnp.zeros(LANES - ROT, f32)])
    ang = positions.astype(f32)[:, None] * inv[None, :]
    sign = jnp.where(jnp.arange(LANES) < half, -1.0, 1.0)
    return jnp.stack([jnp.cos(ang), jnp.sin(ang) * sign])


def chip_ring(chips):
    if chips == 8:
        return [2 * z for z in range(4)] + [2 * z + 1 for z in (3, 2, 1, 0)]
    return list(range(chips))


def order(scal, *firsts):
    for x in firsts:
        scal = scal + (x[(slice(0, 1),) * x.ndim].reshape(()).astype(f32) > 1e30).astype(jnp.int32)
    return scal


def local_fn(qkv, prefix_kv, cache_pool, page_table, cached_lens, span_lens, dense_weight, dense_bias):
    tok, fsdp = lax.axis_size("tok"), lax.axis_size("fsdp")
    span, _, width = qkv.shape
    qkv = jnp.transpose(qkv, (1, 0, 2))
    pool = cache_pool[0]
    max_pages, _, page_len, _ = pool.shape
    prefix_len = prefix_kv.shape[1] * tok
    f = lax.axis_index("fsdp")
    meta = jnp.concatenate([cached_lens, span_lens, page_table[0]])
    rows = jnp.arange(span, dtype=jnp.int32)

    def scalars(m, col, pcol, scol=0):
        return jnp.concatenate([m[:2], jnp.stack([jnp.asarray(x, jnp.int32) for x in (col, pcol, scol)]), m[2:]])

    if width % (2 * GW) or tok % 2 or fsdp != 2:
        table = rotary_angles(prefix_len + meta[0] + rows)
        whole = lax.all_gather(prefix_kv, "tok", axis=1, tiled=True)
        pieces, offsets = [], []
        for g in range(width // GW):
            got = attend(scalars(meta, g * GW, g * GW), span, page_len, max_pages, local=(qkv, pool, table), pieces=[whole])
            every = lax.all_gather(got, "fsdp", axis=0)
            for i in range(fsdp):
                pieces.append(every[i])
                offsets.append(i * width + g * GW)
        return project(meta[1], offsets, pieces, dense_weight, dense_bias[None])

    half = width // 2
    c = lax.axis_index("tok") % 2
    swap_pairs = [(i, i ^ 1) for i in range(tok)]
    ring = chip_ring(tok // 2)
    n = len(ring)
    ahead = [(2 * ring[i] + k, 2 * ring[(i + 1) % n] + k) for i in range(n) for k in range(2)]
    back = [(b, a) for a, b in ahead]

    def swap(x):
        return lax.ppermute(x, "tok", swap_pairs)

    def part(x, which):
        return lax.dynamic_slice_in_dim(x, which * half, half, x.ndim - 1)

    meta2 = swap(meta)
    mine = jnp.concatenate([part(prefix_kv, c), swap(part(prefix_kv, 1 - c))], axis=1)
    hop = {1: (lax.ppermute(mine, "tok", ahead), lax.ppermute(mine, "tok", back))}
    mates = {0: (meta, qkv, pool, rotary_angles(prefix_len + meta[0] + rows))}
    groups = [g * GW for g in range(half // GW)]
    units = [(who, col) for who in (0, 1) for col in groups]
    steps = n // 2
    carries = {}
    for i, (who, col) in enumerate(units):
        m, a, b, t = mates[who]
        s = scalars(m, col if who else c * half + col, col, (1 - c) * half)
        s = s if i else order(s, mine[:, -1:])
        got = attend(s, span, page_len, max_pages, local=(a, b, t), send=0 if i else half)
        if not i:
            mates[1] = (meta2, swap(got[2]), swap(got[3]), rotary_angles(prefix_len + meta2[0] + rows))
        carries[who, col] = got[:2]
        d = i + 2
        if d <= steps:
            fw, bw = hop[d - 1]
            fw, bw, carries[who, col] = lax.optimization_barrier((fw, bw, carries[who, col]))
            hop[d] = (lax.ppermute(fw, "tok", ahead),)
            if d < steps:
                hop[d] += (lax.ppermute(bw, "tok", back),)
    pieces = [mine] + [x for d in range(1, steps + 1) for x in hop[d]]
    ypairs = [(0, 1), (1, 0)]
    proj, offsets, early = [], [], []
    for who, col in [(w, col) for w in (1, 0) for col in groups]:
        s = scalars(mates[who][0], 0, col)
        s = s if who else order(s, *early)
        got = attend(s, span, page_len, max_pages, carry=carries[who, col], pieces=pieces)
        if who:
            early.append(got)
        far = lax.ppermute(got, "fsdp", ypairs)
        if who:
            got, far = swap(got), swap(far)
        at = (1 - c if who else c) * half + col
        proj += [got, far]
        offsets += [f * width + at, (1 - f) * width + at]
    part_sum = project(meta[1], offsets[:-2], proj[:-2], dense_weight, dense_bias[None], last=False)
    return project(meta[1], offsets[-2:], proj[-2:], dense_weight, part_sum)


def solution(mesh):
    return jax.shard_map(
        local_fn,
        mesh=mesh,
        in_specs=(
            P("tok", None, "fsdp"),
            P(None, "tok", "fsdp"),
            P("tok", None, None, None, "fsdp"),
            P("tok", None),
            P("tok"),
            P("tok"),
            P(None, "fsdp"),
            P("fsdp"),
        ),
        out_specs=P("tok", "fsdp"),
        check_vma=False,
    )
```
